256 devices in a mesh: dp: 16 (over z_hi, x), feat: 16 (over y, z_lo, core).
Axes of the slice: x: 4, y: 4, z: 8 (z_hi: 4, z_lo: 2; z = z_hi * 2 + z_lo), core: 2. Of those that a mesh axis runs over, the one named last changes fastest.
Arguments:
- residual: bfloat16 [384, 7168], P('dp'), may hold values from -6 to 6
- cotangent: bfloat16 [384, 7168], P('dp'), may hold values from -6 to 6
- encoder_weight: bfloat16 [7168, 65536], P('dp', 'feat'), may hold values from -0.0625 to 0.0625
- encoder_bias: float32 [65536], P('feat'), may hold values from -3 to 3
- decoder_weight: bfloat16 [65536, 7168], P('feat', 'dp'), may hold values from -0.0625 to 0.0625
- route_experts: int32 [384, 8], P('dp'), may hold values from 0 to 255, all different within a row
- route_buckets: int32 [384, 8], P('dp'), may hold values from 1 to 8
Outputs:
- expert_credit: float32 [256, 65536], P('dp', 'feat')
The draws below stay inside these ranges and needn't reach their ends.
Inputs may be any that keep to these rules, and one draw needn't show every extreme that they name: `route_experts`: each token names 8 different experts, and every expert is named by some token.
All inputs are finite; a program needn't handle non-finite values.
Results may differ from the reference program's by a relative error of at most 0.0003.
Values may be sent and summed in bfloat16 or wider, within the bound.
A program may use at most 128 MiB of HBM per device.

```python
import jax
import jax.numpy as jnp
from jax import lax

D = 7168
E = 256
TOPK = 8
F = 65536
TOKENS = 384


def set_ends(entries, stream_key, least, top_value):
    longest = entries.shape.index(max(entries.shape))
    spots = []
    for shift in (0, 1):
        where = [jax.random.randint(jax.random.fold_in(stream_key, axis), (), 0, length) for axis, length in enumerate(entries.shape)]
        where[longest] = (where[longest] + shift) % entries.shape[longest]
        spots.append(tuple(where))
    return entries.at[spots[0]].set(least).at[spots[1]].set(top_value)


def levels(own_key, extent, split, smallest, high):
    level, own = 1.0, jax.random.fold_in(own_key, 6)
    for position, shards_of in split:
        steps = jnp.exp(jax.random.uniform(jax.random.fold_in(own, position), (shards_of,), jnp.float32, smallest / len(split), high / len(split)))
        level = level * jnp.repeat(steps, extent[position] // shards_of).reshape([-1 if axis == position else 1 for axis in range(len(extent))])
    return level


def picks_of(own_key, rows, number_of, top, lift):
    order = jax.random.permutation(jax.random.fold_in(own_key, 1), number_of)
    favour = order
    for power in range(3):
        favour = favour * favour // number_of
    favour = favour * lift // number_of
    chance = jax.random.randint(jax.random.fold_in(own_key, 2), (rows, number_of), 0, 4096) + favour
    sure = jax.random.permutation(jax.random.fold_in(own_key, 3), rows)[jnp.arange(number_of) % rows]
    chance = jnp.where(jnp.arange(rows)[:, None] == sure[None, :], 1 << 14, chance)
    merit = chance * number_of + jnp.arange(number_of)
    return lax.top_k(merit.astype(jnp.int32), top)[1].astype(jnp.int32)


def gaussian(stream_key, shape, scale, most, split=(), kind=jnp.bfloat16):
    array = jax.random.normal(stream_key, shape, jnp.float32) * scale
    if len(split) > 0:
        array = levels(stream_key, shape, split, -0.22, 0.18) * array
    return jnp.clip(array, min=-most, max=most).astype(kind)


def setup_inputs(seed: int = 0) -> dict:
    streams_of = jax.random.split(jax.random.key(seed), 8)
    return {
        "residual": gaussian(streams_of[0], (TOKENS, D), 1.0, 6.0, ((0, 16),)),
        "cotangent": gaussian(streams_of[1], (TOKENS, D), 1.0, 6.0, ((0, 16),)),
        "encoder_weight": gaussian(streams_of[2], (D, F), D ** -0.5, 0.0625, ((0, 16), (1, 16))),
        "encoder_bias": gaussian(streams_of[3], (F,), 0.5, 3.0, ((0, 16),), jnp.float32),
        "decoder_weight": gaussian(streams_of[4], (F, D), D ** -0.5, 0.0625, ((0, 16), (1, 16))),
        "route_experts": picks_of(streams_of[5], TOKENS, E, TOPK, 256),
        "route_buckets": set_ends(jax.random.randint(streams_of[6], (TOKENS, TOPK), 1, 9), jax.random.fold_in(streams_of[6], 1), 1, 8).astype(jnp.int32),
    }


def reference(residual, cotangent, encoder_weight, encoder_bias, decoder_weight, route_experts, route_buckets):
    pre = jnp.dot(residual.astype(jnp.float32), encoder_weight.astype(jnp.float32), precision=lax.Precision.HIGHEST)
    grad = lax.dot_general(cotangent.astype(jnp.float32), decoder_weight.astype(jnp.float32), (((1,), (1,)), ((), ())), precision=lax.Precision.HIGHEST)
    score = jnp.maximum(pre + encoder_bias[None, :], 0.0) * grad
    expert_ids = jnp.arange(E, dtype=jnp.int32)
    weights = route_buckets.astype(jnp.float32) * 0.125
    routing = jnp.sum((route_experts[:, :, None] == expert_ids[None, None, :]).astype(jnp.float32) * weights[:, :, None], axis=1)
    return lax.dot_general(routing, score, (((0,), (0,)), ((), ())), precision=lax.Precision.HIGHEST)
```

```python
import jax
import jax.numpy as jnp
from jax import lax
from jax.sharding import PartitionSpec as P

E = 256


def routing_table(experts, buckets):
    expert_ids = jnp.arange(E, dtype=jnp.int32)
    weights = buckets.astype(jnp.float32) * 0.125
    return jnp.sum(
        (experts[:, :, None] == expert_ids[None, None, :]).astype(jnp.float32)
        * weights[:, :, None],
        axis=1,
    )


def on_device(
    residual, cotangent, encoder_weight, encoder_bias, decoder_weight, route_experts, route_buckets
):
    rows = lax.all_to_all(residual, "dp", split_axis=1, concat_axis=0, tiled=True)
    tangent = lax.all_to_all(cotangent, "dp", split_axis=1, concat_axis=0, tiled=True)
    routing = lax.all_gather(
        routing_table(route_experts, route_buckets).astype(jnp.bfloat16), "dp", axis=0, tiled=True
    ).astype(jnp.float32)
    pre = jnp.dot(rows, encoder_weight, preferred_element_type=jnp.float32)
    pre = lax.psum_scatter(pre, "dp", scatter_dimension=1, tiled=True)
    grad = lax.dot_general(
        tangent, decoder_weight, (((1,), (1,)), ((), ())), preferred_element_type=jnp.float32
    )
    grad = lax.psum_scatter(grad, "dp", scatter_dimension=1, tiled=True)
    share = pre.shape[1]
    bias = lax.dynamic_slice(encoder_bias, (lax.axis_index("dp") * share,), (share,))
    score = jnp.maximum(pre + bias[None, :], 0.0) * grad
    credit = lax.dot_general(
        routing, score, (((0,), (0,)), ((), ())), precision=lax.Precision.HIGHEST
    )
    return lax.all_to_all(credit, "dp", split_axis=0, concat_axis=1, tiled=True)


def solution(mesh):
    placed = (
        P("dp", None),
        P("dp", None),
        P("dp", "feat"),
        P("feat"),
        P("feat", "dp"),
        P("dp", None),
        P("dp", None),
    )
    return jax.shard_map(
        on_device, mesh=mesh, in_specs=placed, out_specs=P("dp", "feat"), check_vma=False
    )
```

```python
import functools

import jax
import jax.numpy as jnp
from jax import lax
from jax.experimental import pallas as pl
from jax.experimental.pallas import tpu as pltpu
from jax.sharding import PartitionSpec as P

TOKENS = 384
E = 256
RX = 4
NDP = 16
OWN = TOKENS // NDP
WIDE = 512
LIVE = 448
CHUNK = 256
HALF = 128
ROWS = TOKENS + 16
MESH = pl.DeviceIdType.MESH


def encode(values, ref):
    top = jnp.max(jnp.abs(values), axis=0, keepdims=True)
    step = jnp.ceil(jnp.log(jnp.maximum(top, 1e-30)) * 32.0)
    inverse = jnp.exp(step * (-1.0 / 32.0)) * 32000.0
    ref[0:TOKENS, :] = jnp.round(values * inverse).astype(jnp.int32).astype(jnp.int16)
    ref[TOKENS:ROWS, :] = (
        jnp.broadcast_to(step, (16, HALF)).astype(jnp.int32).astype(jnp.int16)
    )


def decode(ref):
    step = ref[TOKENS:ROWS, :].astype(jnp.int32).astype(jnp.float32)[0:1, :]
    scale = jnp.exp(step * (1.0 / 32.0)) * (1.0 / 32000.0)
    return ref[0:TOKENS, :].astype(jnp.int32).astype(jnp.float32) * scale


def window_start(d):
    return 896 * (d // 2) + 384 * (d % 2)


def kernel(
    residual,
    cotangent,
    encoder,
    decoder,
    bias,
    codes,
    out,
    weights,
    landing,
    tokens,
    table,
    near,
    own,
    summed,
    xsend,
    xrecv,
    zsend,
    zrecv,
    credit,
    routing,
    w_sem,
    l_sem,
    tok_send,
    tok_recv,
    sib_send,
    sib_recv,
    tab_send,
    tab_recv,
    xs_sem,
    xr_sem,
    zs_sem,
    zr_sem,
    out_send,
    out_recv,
):
    me = lax.axis_index("dp")
    feat = lax.axis_index("feat")
    core = feat % 2
    sibling = feat + 1 - 2 * core
    x = me % RX
    z = me // RX
    off = 64 * (me % 2)

    x_left = z * RX + (x + 3) % RX
    x_right = z * RX + (x + 1) % RX
    z_left = ((z + 3) % RX) * RX + x
    z_right = ((z + 1) % RX) * RX + x

    def weight_copy(m):
        source = encoder if m == 0 else decoder
        return pltpu.make_async_copy(
            source, weights.at[m, pl.ds(pl.multiple_of(off, 64), LIVE), :], w_sem.at[m]
        )

    for m in range(2):
        weight_copy(m).start()

    columns = pl.ds(pl.multiple_of(core * 256, 256), 256)

    def token_source(m, d):
        source = residual if m == 0 else cotangent
        return source.at[:, pl.ds(pl.multiple_of(window_start(d) + core * 256, 128), 256)]

    def token_local(m):
        return pltpu.make_async_copy(token_source(m, me), landing.at[m, me], l_sem.at[m])

    table_local = pltpu.make_async_copy(codes, table.at[me], l_sem.at[2])
    for m in range(2):
        token_local(m).start()
    table_local.start()

    barrier = pltpu.get_barrier_semaphore()

    def greet(i, carry):
        pl.semaphore_signal(
            barrier, inc=1, device_id={"dp": (me + i) % NDP}, device_id_type=MESH
        )
        return carry

    lax.fori_loop(1, NDP, greet, 0)
    pl.semaphore_signal(barrier, inc=1, device_id={"feat": sibling}, device_id_type=MESH)
    pl.semaphore_wait(barrier, NDP)

    def token_copy(m, i):
        d = (me + i) % NDP
        return pltpu.make_async_remote_copy(
            src_ref=token_source(m, d),
            dst_ref=landing.at[m, me],
            send_sem=tok_send.at[m, i],
            recv_sem=tok_recv.at[m, i],
            device_id={"dp": d},
            device_id_type=MESH,
        )

    def sibling_copy(m):
        part = tokens.at[m, :, columns]
        return pltpu.make_async_remote_copy(
            src_ref=part,
            dst_ref=part,
            send_sem=sib_send.at[m],
            recv_sem=sib_recv.at[m],
            device_id={"feat": sibling},
            device_id_type=MESH,
        )

    def sibling_arrived(m):
        part = tokens.at[m, :, pl.ds(pl.multiple_of(256 - core * 256, 256), 256)]
        return pltpu.make_async_remote_copy(
            src_ref=part,
            dst_ref=part,
            send_sem=sib_send.at[m],
            recv_sem=sib_recv.at[m],
            device_id={"feat": sibling},
            device_id_type=MESH,
        )

    def token_arrived(m, i):
        s = (me + NDP - i) % NDP
        part = landing.at[m, s]
        return pltpu.make_async_remote_copy(
            src_ref=part,
            dst_ref=part,
            send_sem=tok_send.at[m, i],
            recv_sem=tok_recv.at[m, i],
            device_id={"dp": s},
            device_id_type=MESH,
        )

    def table_copy(i):
        d = (me + i) % NDP
        return pltpu.make_async_remote_copy(
            src_ref=codes,
            dst_ref=table.at[me],
            send_sem=tab_send.at[i],
            recv_sem=tab_recv.at[i],
            device_id={"dp": d},
            device_id_type=MESH,
        )

    def table_arrived(i):
        s = (me + NDP - i) % NDP
        part = table.at[s]
        return pltpu.make_async_remote_copy(
            src_ref=part,
            dst_ref=part,
            send_sem=tab_send.at[i],
            recv_sem=tab_recv.at[i],
            device_id={"dp": s},
            device_id_type=MESH,
        )

    def peers(action):
        def step(i, carry):
            action(i)
            return carry

        lax.fori_loop(1, NDP, step, 0)

    for m in range(2):
        peers(lambda i, m=m: token_copy(m, i).start())
    peers(lambda i: table_copy(i).start())

    blank = pl.ds(pl.multiple_of(LIVE - LIVE * (me % 2), 64), 64)
    for m in range(2):
        weights[m, blank, :] = jnp.zeros((64, weights.shape[2]), jnp.bfloat16)

    def tokens_ready(m):
        token_local(m).wait()
        peers(lambda i: token_arrived(m, i).wait_recv())
        rows = landing[m].astype(jnp.float32).reshape(TOKENS, 256)
        tokens[m, :, columns] = rows.astype(jnp.bfloat16)
        sibling_copy(m).start()
        weight_copy(m).wait()
        sibling_arrived(m).wait_recv()

    def x_copy(u, j):
        return pltpu.make_async_remote_copy(
            src_ref=xsend.at[u, j],
            dst_ref=xrecv.at[u, j],
            send_sem=xs_sem.at[u, j],
            recv_sem=xr_sem.at[u, j],
            device_id={"dp": x_left if j % 2 == 0 else x_right},
            device_id_type=MESH,
        )

    def z_copy(m, j):
        return pltpu.make_async_remote_copy(
            src_ref=zsend.at[m, j],
            dst_ref=zrecv.at[m, j],
            send_sem=zs_sem.at[m, j],
            recv_sem=zr_sem.at[m, j],
            device_id={"dp": z_left if j % 2 == 0 else z_right},
            device_id_type=MESH,
        )

    def x_send(u, j, values):
        encode(values, xsend.at[u, j])
        x_copy(u, j).start()

    def z_send(m, j, values):
        encode(values, zsend.at[m, j])
        z_copy(m, j).start()

    def produce(u):
        k, m = u // 2, u % 2
        back = 3 - k
        row = (z + ((back + 1) % 3 + 1) * ((back + 3) // 4)) % RX

        def partial(hop):
            block = row * RX + (x + hop) % RX
            return jnp.dot(
                tokens[m],
                weights[m, :, pl.ds(pl.multiple_of(block * CHUNK, CHUNK), CHUNK)],
                preferred_element_type=jnp.float32,
            )

        far = partial(2)
        x_send(u, 0, far[:, :HALF])
        x_send(u, 1, far[:, HALF:])
        left = partial(3)
        x_send(u, 2, left[:, HALF:])
        near[u, 0] = left[:, :HALF]
        right = partial(1)
        x_send(u, 3, right[:, :HALF])
        near[u, 1] = right[:, HALF:]
        own[u] = partial(0)

    def combine(u):
        for j in range(2):
            x_copy(u, j).wait_recv()
            x_send(u, 4 + j, near[u, j] + decode(xrecv.at[u, j]))

    def x_total(u):
        for j in range(2, 6):
            x_copy(u, j).wait_recv()
        first = own[u, :, :HALF] + decode(xrecv.at[u, 4]) + decode(xrecv.at[u, 3])
        second = own[u, :, HALF:] + decode(xrecv.at[u, 5]) + decode(xrecv.at[u, 2])
        return first, second

    def finish(u):
        k, m = u // 2, u % 2
        first, second = x_total(u)
        summed[0] = first
        summed[1] = second

        @pl.when(k == 0)
        def _():
            z_send(m, 0, summed[0])
            z_send(m, 1, summed[1])

        @pl.when(k == 1)
        def _():
            z_send(m, 3, summed[0])
            z_copy(m, 1).wait_recv()
            z_send(m, 5, summed[1] + decode(zrecv.at[m, 1]))

        @pl.when(k == 2)
        def _():
            z_send(m, 2, summed[1])
            z_copy(m, 0).wait_recv()
            z_send(m, 4, summed[0] + decode(zrecv.at[m, 0]))

        @pl.when(k == 3)
        def _():
            for j in range(2, 6):
                z_copy(m, j).wait_recv()
            near[m, 0] = summed[0] + decode(zrecv.at[m, 4]) + decode(zrecv.at[m, 3])
            near[m, 1] = summed[1] + decode(zrecv.at[m, 5]) + decode(zrecv.at[m, 2])

    def build_routing():
        table_local.wait()
        peers(lambda i: table_arrived(i).wait_recv())
        values = table[...].astype(jnp.float32).reshape(TOKENS, HALF)
        experts = lax.broadcasted_iota(jnp.int32, (TOKENS, E), 1).astype(jnp.float32)
        total = jnp.zeros((TOKENS, E), jnp.float32)
        for k in range(8):
            total += jnp.where(values[:, k : k + 1] == experts, values[:, 8 + k : 9 + k], 0.0)
        routing[...] = total.astype(jnp.bfloat16)

    def step(u, carry):
        @pl.when(u < 2)
        def _():
            tokens_ready_any(u)

        @pl.when(u < 8)
        def _():
            produce(u)

        @pl.when(u == 2)
        def _():
            build_routing()

        @pl.when((u >= 1) & (u < 9))
        def _():
            combine(u - 1)

        @pl.when(u >= 2)
        def _():
            finish(u - 2)

        return carry

    def tokens_ready_any(u):
        @pl.when(u == 0)
        def _():
            tokens_ready(0)

        @pl.when(u == 1)
        def _():
            tokens_ready(1)

    lax.fori_loop(0, 10, step, 0)

    for h in range(2):
        level = bias[:, pl.ds(pl.multiple_of(me * CHUNK + h * HALF, HALF), HALF)]
        score = jnp.maximum(near[0, h] + level, 0.0) * near[1, h]
        high = score.astype(jnp.bfloat16)
        low = (score - high.astype(jnp.float32)).astype(jnp.bfloat16)
        over_tokens = (((0,), (0,)), ((), ()))
        part = lax.dot_general(
            routing[...], high, over_tokens, preferred_element_type=jnp.float32
        ) + lax.dot_general(routing[...], low, over_tokens, preferred_element_type=jnp.float32)
        credit[:, h * HALF : (h + 1) * HALF] = part

    mine = pl.ds(pl.multiple_of(me * CHUNK, CHUNK), CHUNK)

    def out_copy(i):
        d = (me + i) % NDP
        return pltpu.make_async_remote_copy(
            src_ref=credit.at[pl.ds(pl.multiple_of(d * 16, 16), 16), :],
            dst_ref=out.at[:, mine],
            send_sem=out_send.at[i],
            recv_sem=out_recv.at[i],
            device_id={"dp": d},
            device_id_type=MESH,
        )

    def out_arrived(i):
        s = (me + NDP - i) % NDP
        part = out.at[:, pl.ds(pl.multiple_of(s * CHUNK, CHUNK), CHUNK)]
        return pltpu.make_async_remote_copy(
            src_ref=part,
            dst_ref=part,
            send_sem=out_send.at[i],
            recv_sem=out_recv.at[i],
            device_id={"dp": s},
            device_id_type=MESH,
        )

    peers(lambda i: out_copy(i).start())
    out[:, mine] = credit[pl.ds(pl.multiple_of(me * 16, 16), 16), :]

    for m in range(2):
        peers(lambda i, m=m: token_copy(m, i).wait_send())
        sibling_copy(m).wait_send()
    peers(lambda i: table_copy(i).wait_send())

    def x_sent(u, carry):
        for j in range(6):
            x_copy(u, j).wait_send()
        return carry

    def z_sent(m, carry):
        for j in range(6):
            z_copy(m, j).wait_send()
        return carry

    lax.fori_loop(0, 8, x_sent, 0)
    lax.fori_loop(0, 2, z_sent, 0)
    peers(lambda i: out_arrived(i).wait_recv())
    peers(lambda i: out_copy(i).wait_send())


def on_device(
    residual, cotangent, encoder_weight, encoder_bias, decoder_weight, route_experts, route_buckets
):
    codes = jnp.concatenate(
        [
            route_experts.astype(jnp.bfloat16),
            (route_buckets.astype(jnp.float32) * 0.125).astype(jnp.bfloat16),
            jnp.zeros((OWN, HALF - 16), jnp.bfloat16),
        ],
        axis=1,
    )
    features = encoder_bias.shape[0]
    vmem = pl.BlockSpec(memory_space=pltpu.VMEM)
    hbm = pl.BlockSpec(memory_space=pl.ANY)
    dma = pltpu.SemaphoreType.DMA
    return pl.pallas_call(
        kernel,
        out_shape=jax.ShapeDtypeStruct((E // NDP, features), jnp.float32),
        in_specs=[hbm, hbm, hbm, hbm, vmem, vmem],
        out_specs=vmem,
        scratch_shapes=[
            pltpu.VMEM((2, WIDE, features), jnp.bfloat16),
            pltpu.VMEM((2, NDP, OWN, 256), jnp.bfloat16),
            pltpu.VMEM((2, TOKENS, WIDE), jnp.bfloat16),
            pltpu.VMEM((NDP, OWN, HALF), jnp.bfloat16),
            pltpu.VMEM((8, 2, TOKENS, HALF), jnp.float32),
            pltpu.VMEM((8, TOKENS, CHUNK), jnp.float32),
            pltpu.VMEM((2, TOKENS, HALF), jnp.float32),
            pltpu.VMEM((8, 6, ROWS, HALF), jnp.int16),
            pltpu.VMEM((8, 6, ROWS, HALF), jnp.int16),
            pltpu.VMEM((2, 6, ROWS, HALF), jnp.int16),
            pltpu.VMEM((2, 6, ROWS, HALF), jnp.int16),
            pltpu.VMEM((E, CHUNK), jnp.float32),
            pltpu.VMEM((TOKENS, E), jnp.bfloat16),
            dma((2,)),
            dma((3,)),
            dma((2, NDP)),
            dma((2, NDP)),
            dma((2,)),
            dma((2,)),
            dma((NDP,)),
            dma((NDP,)),
            dma((8, 6)),
            dma((8, 6)),
            dma((2, 6)),
            dma((2, 6)),
            dma((NDP,)),
            dma((NDP,)),
        ],
        compiler_params=pltpu.CompilerParams(
            collective_id=0, has_side_effects=True, vmem_limit_bytes=56 * 1024 * 1024
        ),
        name="credit",
    )(
        residual,
        cotangent,
        encoder_weight,
        decoder_weight.T,
        encoder_bias.reshape(1, features),
        codes,
    )


def solution(mesh):
    placed = (
        P("dp", None),
        P("dp", None),
        P("dp", "feat"),
        P("feat"),
        P("feat", "dp"),
        P("dp", None),
        P("dp", None),
    )
    return jax.shard_map(
        on_device, mesh=mesh, in_specs=placed, out_specs=P("dp", "feat"), check_vma=False
    )
```

```python
import functools

import jax
import jax.numpy as jnp
from jax import lax
from jax.experimental import pallas as pl
from jax.experimental.pallas import tpu as pltpu
from jax.sharding import PartitionSpec as P

TOKENS = 384
E = 256
RX = 4
NDP = 16
OWN = TOKENS // NDP
WIDE = 512
LIVE = 448
CHUNK = 256
HALF = 128
SPAN = TOKENS // 2
ROWS = SPAN + 8
UNITS = 16
MESH = pl.DeviceIdType.MESH


def encode(values, ref):
    top = jnp.max(jnp.abs(values), axis=0, keepdims=True)
    step = jnp.ceil(jnp.log(jnp.maximum(top, 1e-30)) * 32.0)
    inverse = jnp.exp(step * (-1.0 / 32.0)) * 32000.0
    ref[0:SPAN, :] = jnp.round(values * inverse).astype(jnp.int32).astype(jnp.int16)
    ref[SPAN:ROWS, :] = jnp.broadcast_to(step, (8, HALF)).astype(jnp.int32).astype(jnp.int16)


def decode(ref):
    step = ref[SPAN:ROWS, :].astype(jnp.int32).astype(jnp.float32)[0:1, :]
    scale = jnp.exp(step * (1.0 / 32.0)) * (1.0 / 32000.0)
    return ref[0:SPAN, :].astype(jnp.int32).astype(jnp.float32) * scale


def window_start(d):
    return 896 * (d // 2) + 384 * (d % 2)


def kernel(
    residual,
    cotangent,
    encoder,
    decoder,
    bias_hbm,
    experts_hbm,
    buckets_hbm,
    out,
    weights,
    landing,
    tokens,
    table,
    bias,
    experts,
    buckets,
    codes,
    near,
    own,
    final,
    xsend,
    xrecv,
    zsend,
    zrecv,
    credit,
    routing,
    w_sem,
    l_sem,
    tok_send,
    tok_recv,
    sib_send,
    sib_recv,
    tab_send,
    tab_recv,
    xs_sem,
    xr_sem,
    zs_sem,
    zr_sem,
    out_send,
    out_recv,
):
    me = lax.axis_index("dp")
    feat = lax.axis_index("feat")
    core = feat % 2
    sibling = feat + 1 - 2 * core
    x = me % RX
    z = me // RX
    off = 64 * (me % 2)

    x_left = z * RX + (x + 3) % RX
    x_right = z * RX + (x + 1) % RX
    z_left = ((z + 3) % RX) * RX + x
    z_right = ((z + 1) % RX) * RX + x

    def weight_copy(m):
        source = encoder if m == 0 else decoder
        return pltpu.make_async_copy(
            source, weights.at[m, pl.ds(pl.multiple_of(off, 64), LIVE), :], w_sem.at[m]
        )

    for m in range(2):
        weight_copy(m).start()

    columns = pl.ds(pl.multiple_of(core * 256, 256), 256)

    def token_source(m, d):
        source = residual if m == 0 else cotangent
        return source.at[:, pl.ds(pl.multiple_of(window_start(d) + core * 256, 128), 256)]

    def token_local(m):
        return pltpu.make_async_copy(token_source(m, me), landing.at[m, me], l_sem.at[m])

    small = [
        pltpu.make_async_copy(source, target, l_sem.at[3 + n])
        for n, (source, target) in enumerate(
            ((bias_hbm, bias), (experts_hbm, experts), (buckets_hbm, buckets))
        )
    ]
    for m in range(2):
        token_local(m).start()
    for copy in small:
        copy.start()

    barrier = pltpu.get_barrier_semaphore()

    def greet(i, carry):
        pl.semaphore_signal(
            barrier, inc=1, device_id={"dp": (me + i) % NDP}, device_id_type=MESH
        )
        return carry

    lax.fori_loop(1, NDP, greet, 0)
    pl.semaphore_signal(barrier, inc=1, device_id={"feat": sibling}, device_id_type=MESH)
    pl.semaphore_wait(barrier, NDP)

    def token_copy(m, i):
        d = (me + i) % NDP
        return pltpu.make_async_remote_copy(
            src_ref=token_source(m, d),
            dst_ref=landing.at[m, me],
            send_sem=tok_send.at[m, i],
            recv_sem=tok_recv.at[m, i],
            device_id={"dp": d},
            device_id_type=MESH,
        )

    def sibling_copy(m):
        part = tokens.at[m, :, columns]
        return pltpu.make_async_remote_copy(
            src_ref=part,
            dst_ref=part,
            send_sem=sib_send.at[m],
            recv_sem=sib_recv.at[m],
            device_id={"feat": sibling},
            device_id_type=MESH,
        )

    def sibling_arrived(m):
        part = tokens.at[m, :, pl.ds(pl.multiple_of(256 - core * 256, 256), 256)]
        return pltpu.make_async_remote_copy(
            src_ref=part,
            dst_ref=part,
            send_sem=sib_send.at[m],
            recv_sem=sib_recv.at[m],
            device_id={"feat": sibling},
            device_id_type=MESH,
        )

    def token_arrived(m, i):
        s = (me + NDP - i) % NDP
        part = landing.at[m, s]
        return pltpu.make_async_remote_copy(
            src_ref=part,
            dst_ref=part,
            send_sem=tok_send.at[m, i],
            recv_sem=tok_recv.at[m, i],
            device_id={"dp": s},
            device_id_type=MESH,
        )

    def table_copy(i):
        d = (me + i) % NDP
        return pltpu.make_async_remote_copy(
            src_ref=codes,
            dst_ref=table.at[me],
            send_sem=tab_send.at[i],
            recv_sem=tab_recv.at[i],
            device_id={"dp": d},
            device_id_type=MESH,
        )

    def table_arrived(i):
        s = (me + NDP - i) % NDP
        part = table.at[s]
        return pltpu.make_async_remote_copy(
            src_ref=part,
            dst_ref=part,
            send_sem=tab_send.at[i],
            recv_sem=tab_recv.at[i],
            device_id={"dp": s},
            device_id_type=MESH,
        )

    def peers(action):
        def step(i, carry):
            action(i)
            return carry

        lax.fori_loop(1, NDP, step, 0)

    for m in range(2):
        peers(lambda i, m=m: token_copy(m, i).start())

    for copy in small:
        copy.wait()
    codes[...] = jnp.zeros_like(codes)
    named = experts[...].astype(jnp.float32)
    weight = buckets[...].astype(jnp.float32) * 0.125
    both = jnp.concatenate([named, weight], axis=0).astype(jnp.bfloat16)
    same = lax.broadcasted_iota(jnp.int32, (OWN, OWN), 0) == lax.broadcasted_iota(
        jnp.int32, (OWN, OWN), 1
    )
    codes[:, 0:16] = lax.dot_general(
        jnp.where(same, 1.0, 0.0).astype(jnp.bfloat16),
        both,
        (((1,), (1,)), ((), ())),
        preferred_element_type=jnp.float32,
    ).astype(jnp.bfloat16)
    table_local = pltpu.make_async_copy(codes, table.at[me], l_sem.at[2])
    table_local.start()

    blank = pl.ds(pl.multiple_of(LIVE - LIVE * (me % 2), 64), 64)
    for m in range(2):
        weights[m, blank, :] = jnp.zeros((64, weights.shape[2]), jnp.bfloat16)

    def tokens_ready(m):
        token_local(m).wait()
        peers(lambda i: token_arrived(m, i).wait_recv())
        rows = landing[m].astype(jnp.float32).reshape(TOKENS, 256)
        tokens[m, :, columns] = rows.astype(jnp.bfloat16)
        sibling_copy(m).start()
        weight_copy(m).wait()
        sibling_arrived(m).wait_recv()

    def x_copy(u, j):
        return pltpu.make_async_remote_copy(
            src_ref=xsend.at[u, j],
            dst_ref=xrecv.at[u, j],
            send_sem=xs_sem.at[u, j],
            recv_sem=xr_sem.at[u, j],
            device_id={"dp": x_left if j % 2 == 0 else x_right},
            device_id_type=MESH,
        )

    def z_copy(m, j):
        return pltpu.make_async_remote_copy(
            src_ref=zsend.at[m, j],
            dst_ref=zrecv.at[m, j],
            send_sem=zs_sem.at[m, j],
            recv_sem=zr_sem.at[m, j],
            device_id={"dp": z_left if j % 2 == 0 else z_right},
            device_id_type=MESH,
        )

    def x_send(u, j, values):
        encode(values, xsend.at[u, j])
        x_copy(u, j).start()

    def z_send(m, j, values):
        encode(values, zsend.at[m, j])
        z_copy(m, j).start()

    spans = (pl.ds(0, SPAN), pl.ds(SPAN, SPAN))

    def produce(u):
        k, h, m = u // 4, (u // 2) % 2, u % 2
        back = 3 - k
        row = (z + ((back + 1) % 3 + 1) * ((back + 3) // 4)) % RX

        def partial(hop, part):
            first = (row * RX + (x + hop) % RX) * CHUNK + h * HALF
            return jnp.dot(
                tokens[m, part, :],
                weights[m, :, pl.ds(pl.multiple_of(first, HALF), HALF)],
                preferred_element_type=jnp.float32,
            )

        x_send(u, 0, partial(2, spans[0]))
        x_send(u, 1, partial(2, spans[1]))
        x_send(u, 2, partial(3, spans[1]))
        x_send(u, 3, partial(1, spans[0]))
        near[u, 0] = partial(3, spans[0])
        near[u, 1] = partial(1, spans[1])
        own[u, 0] = partial(0, spans[0])
        own[u, 1] = partial(0, spans[1])

    def combine(u):
        for j in range(2):
            x_copy(u, j).wait_recv()
            x_send(u, 4 + j, near[u, j] + decode(xrecv.at[u, j]))

    def finish(u):
        k, q = u // 4, u % 4
        for j in range(2, 6):
            x_copy(u, j).wait_recv()
        own[u, 0] += decode(xrecv.at[u, 4]) + decode(xrecv.at[u, 3])
        own[u, 1] += decode(xrecv.at[u, 5]) + decode(xrecv.at[u, 2])

        @pl.when(k == 0)
        def _():
            z_send(q, 0, own[u, 0])
            z_send(q, 1, own[u, 1])

        @pl.when(k == 1)
        def _():
            z_send(q, 3, own[u, 0])
            z_copy(q, 1).wait_recv()
            z_send(q, 5, own[u, 1] + decode(zrecv.at[q, 1]))

        @pl.when(k == 2)
        def _():
            z_send(q, 2, own[u, 1])
            z_copy(q, 0).wait_recv()
            z_send(q, 4, own[u, 0] + decode(zrecv.at[q, 0]))

        @pl.when(k == 3)
        def _():
            for j in range(2, 6):
                z_copy(q, j).wait_recv()
            final[q % 2, spans[0], :] = (
                own[u, 0] + decode(zrecv.at[q, 4]) + decode(zrecv.at[q, 3])
            )
            final[q % 2, spans[1], :] = (
                own[u, 1] + decode(zrecv.at[q, 5]) + decode(zrecv.at[q, 2])
            )

        @pl.when((k == 3) & (q % 2 == 1))
        def _():
            deliver(q // 2)

    def build_routing():
        peers(lambda i: table_arrived(i).wait_recv())
        values = table[...].astype(jnp.float32).reshape(TOKENS, HALF).T
        names = lax.broadcasted_iota(jnp.int32, (E, TOKENS), 0).astype(jnp.float32)
        total = jnp.zeros((E, TOKENS), jnp.float32)
        for k in range(8):
            total += jnp.where(values[k : k + 1, :] == names, values[8 + k : 9 + k, :], 0.0)
        routing[...] = total.astype(jnp.bfloat16)

    def out_copy(h, i):
        d = (me + i) % NDP
        return pltpu.make_async_remote_copy(
            src_ref=credit.at[h, pl.ds(pl.multiple_of(d * 16, 16), 16), :],
            dst_ref=out.at[:, pl.ds(pl.multiple_of(me * CHUNK + h * HALF, HALF), HALF)],
            send_sem=out_send.at[h, i],
            recv_sem=out_recv.at[h, i],
            device_id={"dp": d},
            device_id_type=MESH,
        )

    def out_arrived(h, i):
        s = (me + NDP - i) % NDP
        part = out.at[:, pl.ds(pl.multiple_of(s * CHUNK + h * HALF, HALF), HALF)]
        return pltpu.make_async_remote_copy(
            src_ref=part,
            dst_ref=part,
            send_sem=out_send.at[h, i],
            recv_sem=out_recv.at[h, i],
            device_id={"dp": s},
            device_id_type=MESH,
        )

    def deliver(h):
        mine = pl.ds(pl.multiple_of(me * CHUNK + h * HALF, HALF), HALF)
        score = jnp.maximum(final[0] + bias[:, mine], 0.0) * final[1]
        high = score.astype(jnp.bfloat16)
        low = (score - high.astype(jnp.float32)).astype(jnp.bfloat16)
        credit[h] = jnp.dot(
            routing[...], high, preferred_element_type=jnp.float32
        ) + jnp.dot(routing[...], low, preferred_element_type=jnp.float32)
        peers(lambda i: out_copy(h, i).start())
        out[:, mine] = credit[h, pl.ds(pl.multiple_of(me * 16, 16), 16), :]

    def step(u, carry):
        @pl.when(u == 0)
        def _():
            tokens_ready(0)

        @pl.when(u == 1)
        def _():
            tokens_ready(1)
            table_local.wait()
            peers(lambda i: table_copy(i).start())

        @pl.when(u < UNITS)
        def _():
            produce(u)

        @pl.when(u == 4)
        def _():
            build_routing()

        @pl.when((u >= 1) & (u < UNITS + 1))
        def _():
            combine(u - 1)

        @pl.when(u >= 2)
        def _():
            finish(u - 2)

        return carry

    lax.fori_loop(0, UNITS + 2, step, 0)

    for m in range(2):
        peers(lambda i, m=m: token_copy(m, i).wait_send())
        sibling_copy(m).wait_send()
    peers(lambda i: table_copy(i).wait_send())

    def x_sent(u, carry):
        for j in range(6):
            x_copy(u, j).wait_send()
        return carry

    def z_sent(m, carry):
        for j in range(6):
            z_copy(m, j).wait_send()
        return carry

    lax.fori_loop(0, UNITS, x_sent, 0)
    lax.fori_loop(0, 4, z_sent, 0)
    for h in range(2):
        peers(lambda i, h=h: out_arrived(h, i).wait_recv())
        peers(lambda i, h=h: out_copy(h, i).wait_send())


def on_device(
    residual, cotangent, encoder_weight, encoder_bias, decoder_weight, route_experts, route_buckets
):
    features = encoder_bias.shape[0]
    vmem = pl.BlockSpec(memory_space=pltpu.VMEM)
    hbm = pl.BlockSpec(memory_space=pltpu.HBM)
    dma = pltpu.SemaphoreType.DMA
    return pl.pallas_call(
        kernel,
        out_shape=jax.ShapeDtypeStruct((E // NDP, features), jnp.float32),
        in_specs=[hbm] * 7,
        out_specs=vmem,
        scratch_shapes=[
            pltpu.VMEM((2, WIDE, features), jnp.bfloat16),
            pltpu.VMEM((2, NDP, OWN, 256), jnp.bfloat16),
            pltpu.VMEM((2, TOKENS, WIDE), jnp.bfloat16),
            pltpu.VMEM((NDP, OWN, HALF), jnp.bfloat16),
            pltpu.VMEM((1, features), jnp.float32),
            pltpu.VMEM((8, OWN), jnp.int32),
            pltpu.VMEM((8, OWN), jnp.int32),
            pltpu.VMEM((OWN, HALF), jnp.bfloat16),
            pltpu.VMEM((UNITS, 2, SPAN, HALF), jnp.float32),
            pltpu.VMEM((UNITS, 2, SPAN, HALF), jnp.float32),
            pltpu.VMEM((2, TOKENS, HALF), jnp.float32),
            pltpu.VMEM((UNITS, 6, ROWS, HALF), jnp.int16),
            pltpu.VMEM((UNITS, 6, ROWS, HALF), jnp.int16),
            pltpu.VMEM((4, 6, ROWS, HALF), jnp.int16),
            pltpu.VMEM((4, 6, ROWS, HALF), jnp.int16),
            pltpu.VMEM((2, E, HALF), jnp.float32),
            pltpu.VMEM((E, TOKENS), jnp.bfloat16),
            dma((2,)),
            dma((6,)),
            dma((2, NDP)),
            dma((2, NDP)),
            dma((2,)),
            dma((2,)),
            dma((NDP,)),
            dma((NDP,)),
            dma((UNITS, 6)),
            dma((UNITS, 6)),
            dma((4, 6)),
            dma((4, 6)),
            dma((2, NDP)),
            dma((2, NDP)),
        ],
        compiler_params=pltpu.CompilerParams(
            collective_id=0, has_side_effects=True, vmem_limit_bytes=56 * 1024 * 1024
        ),
        name="credit",
    )(
        residual,
        cotangent,
        encoder_weight,
        decoder_weight.T,
        encoder_bias.reshape(1, features),
        route_experts.T,
        route_buckets.T,
    )


def solution(mesh):
    placed = (
        P("dp", None),
        P("dp", None),
        P("dp", "feat"),
        P("feat"),
        P("feat", "dp"),
        P("dp", None),
        P("dp", None),
    )
    return jax.shard_map(
        on_device, mesh=mesh, in_specs=placed, out_specs=P("dp", "feat"), check_vma=False
    )
```

```python
import functools

import jax
import jax.numpy as jnp
from jax import lax
from jax.experimental import pallas as pl
from jax.experimental.pallas import tpu as pltpu
from jax.sharding import PartitionSpec as P

TOKENS = 384
E = 256
RX = 4
NDP = 16
OWN = TOKENS // NDP
WIDE = 512
LIVE = 448
CHUNK = 256
HALF = 128
SPAN = TOKENS // 2
ROWS = SPAN + 8
UNITS = 16
BLOCK = TOKENS // RX
MESH = pl.DeviceIdType.MESH


def encode(values, ref):
    count = values.shape[0]
    top = jnp.max(jnp.abs(values), axis=0, keepdims=True)
    step = jnp.ceil(jnp.log(jnp.maximum(top, 1e-30)) * 32.0)
    inverse = jnp.exp(step * (-1.0 / 32.0)) * 32000.0
    ref[0:count, :] = jnp.round(values * inverse).astype(jnp.int32).astype(jnp.int16)
    ref[count : count + 8, :] = (
        jnp.broadcast_to(step, (8, HALF)).astype(jnp.int32).astype(jnp.int16)
    )


def decode(ref):
    count = ref.shape[0] - 8
    step = ref[count : count + 8, :].astype(jnp.int32).astype(jnp.float32)[0:1, :]
    scale = jnp.exp(step * (1.0 / 32.0)) * (1.0 / 32000.0)
    return ref[0:count, :].astype(jnp.int32).astype(jnp.float32) * scale


def window_start(d):
    return 896 * (d // 2) + 384 * (d % 2)


def kernel(
    residual,
    cotangent,
    encoder,
    decoder,
    bias_hbm,
    experts_hbm,
    buckets_hbm,
    out,
    weights,
    landing,
    tokens,
    table,
    bias,
    experts,
    buckets,
    codes,
    near,
    near_block,
    own,
    final,
    bsend,
    brecv,
    xsend,
    xrecv,
    zsend,
    zrecv,
    credit,
    routing,
    w_sem,
    l_sem,
    tok_send,
    tok_recv,
    sib_send,
    sib_recv,
    sibb_send,
    sibb_recv,
    tab_send,
    tab_recv,
    bs_sem,
    br_sem,
    xs_sem,
    xr_sem,
    zs_sem,
    zr_sem,
    out_send,
    out_recv,
):
    me = lax.axis_index("dp")
    feat = lax.axis_index("feat")
    core = feat % 2
    sibling = feat + 1 - 2 * core
    x = me % RX
    z = me // RX
    off = 64 * (me % 2)

    x_left = z * RX + (x + 3) % RX
    x_right = z * RX + (x + 1) % RX
    z_left = ((z + 3) % RX) * RX + x
    z_right = ((z + 1) % RX) * RX + x

    def weight_copy(m):
        source = encoder if m == 0 else decoder
        return pltpu.make_async_copy(
            source, weights.at[m, pl.ds(pl.multiple_of(off, 64), LIVE), :], w_sem.at[m]
        )

    for m in range(2):
        weight_copy(m).start()

    columns = pl.ds(pl.multiple_of(core * 256, 256), 256)

    def token_source(m, d):
        source = residual if m == 0 else cotangent
        return source.at[:, pl.ds(pl.multiple_of(window_start(d) + core * 256, 128), 256)]

    def token_local(m):
        return pltpu.make_async_copy(token_source(m, me), landing.at[m, me], l_sem.at[m])

    small = [
        pltpu.make_async_copy(source, target, l_sem.at[3 + n])
        for n, (source, target) in enumerate(
            ((bias_hbm, bias), (experts_hbm, experts), (buckets_hbm, buckets))
        )
    ]
    for m in range(2):
        token_local(m).start()
    for copy in small:
        copy.start()

    barrier = pltpu.get_barrier_semaphore()

    def greet(i, carry):
        pl.semaphore_signal(
            barrier, inc=1, device_id={"dp": (me + i) % NDP}, device_id_type=MESH
        )
        return carry

    lax.fori_loop(1, NDP, greet, 0)
    pl.semaphore_signal(barrier, inc=1, device_id={"feat": sibling}, device_id_type=MESH)
    pl.semaphore_wait(barrier, NDP)

    def token_copy(m, i):
        d = (me + i) % NDP
        return pltpu.make_async_remote_copy(
            src_ref=token_source(m, d),
            dst_ref=landing.at[m, me],
            send_sem=tok_send.at[m, i],
            recv_sem=tok_recv.at[m, i],
            device_id={"dp": d},
            device_id_type=MESH,
        )

    def sibling_copy(m):
        part = tokens.at[m, :, columns]
        return pltpu.make_async_remote_copy(
            src_ref=part,
            dst_ref=part,
            send_sem=sib_send.at[m],
            recv_sem=sib_recv.at[m],
            device_id={"feat": sibling},
            device_id_type=MESH,
        )

    def sibling_arrived(m):
        part = tokens.at[m, :, pl.ds(pl.multiple_of(256 - core * 256, 256), 256)]
        return pltpu.make_async_remote_copy(
            src_ref=part,
            dst_ref=part,
            send_sem=sib_send.at[m],
            recv_sem=sib_recv.at[m],
            device_id={"feat": sibling},
            device_id_type=MESH,
        )

    def token_arrived(m, i):
        s = (me + NDP - i) % NDP
        part = landing.at[m, s]
        return pltpu.make_async_remote_copy(
            src_ref=part,
            dst_ref=part,
            send_sem=tok_send.at[m, i],
            recv_sem=tok_recv.at[m, i],
            device_id={"dp": s},
            device_id_type=MESH,
        )

    def table_copy(i):
        d = (me + i) % NDP
        return pltpu.make_async_remote_copy(
            src_ref=codes,
            dst_ref=table.at[me],
            send_sem=tab_send.at[i],
            recv_sem=tab_recv.at[i],
            device_id={"dp": d},
            device_id_type=MESH,
        )

    def table_arrived(i):
        s = (me + NDP - i) % NDP
        part = table.at[s]
        return pltpu.make_async_remote_copy(
            src_ref=part,
            dst_ref=part,
            send_sem=tab_send.at[i],
            recv_sem=tab_recv.at[i],
            device_id={"dp": s},
            device_id_type=MESH,
        )

    def peers(action):
        def step(i, carry):
            action(i)
            return carry

        lax.fori_loop(1, NDP, step, 0)

    def row_offset(t):
        return t + t // 2 - 2 * (t // 3)

    def place(t, hop):
        d = ((z + row_offset(t)) % RX) * RX + (x + hop) % RX
        return (d + NDP - me) % NDP

    for m in range(2):
        for hop in range(1, RX):
            token_copy(m, place(0, hop)).start()

        def send_row(t, carry, m=m):
            for hop in range(RX):
                token_copy(m, place(t, hop)).start()
            return carry

        lax.fori_loop(1, RX, send_row, 0)

    for copy in small:
        copy.wait()
    codes[...] = jnp.zeros_like(codes)
    named = experts[...].astype(jnp.float32)
    weight = buckets[...].astype(jnp.float32) * 0.125
    both = jnp.concatenate([named, weight], axis=0).astype(jnp.bfloat16)
    same = lax.broadcasted_iota(jnp.int32, (OWN, OWN), 0) == lax.broadcasted_iota(
        jnp.int32, (OWN, OWN), 1
    )
    codes[:, 0:16] = lax.dot_general(
        jnp.where(same, 1.0, 0.0).astype(jnp.bfloat16),
        both,
        (((1,), (1,)), ((), ())),
        preferred_element_type=jnp.float32,
    ).astype(jnp.bfloat16)
    table_local = pltpu.make_async_copy(codes, table.at[me], l_sem.at[2])
    table_local.start()

    blank = pl.ds(pl.multiple_of(LIVE - LIVE * (me % 2), 64), 64)
    for m in range(2):
        weights[m, blank, :] = jnp.zeros((64, weights.shape[2]), jnp.bfloat16)

    def block_rows(t):
        return pl.ds(pl.multiple_of(((z + row_offset(t)) % RX) * BLOCK, BLOCK), BLOCK)

    def block_copy(t, part):
        return pltpu.make_async_remote_copy(
            src_ref=part,
            dst_ref=part,
            send_sem=sibb_send.at[t],
            recv_sem=sibb_recv.at[t],
            device_id={"feat": sibling},
            device_id_type=MESH,
        )

    theirs = pl.ds(pl.multiple_of(256 - core * 256, 256), 256)

    def block_share(t):
        for hop in range(RX):
            s = ((z + row_offset(t)) % RX) * RX + (x + hop) % RX
            if hop == 0:

                @pl.when(t > 0)
                def _():
                    token_arrived(0, (me + NDP - s) % NDP).wait_recv()

                @pl.when(t == 0)
                def _():
                    token_local(0).wait()
            else:
                token_arrived(0, (me + NDP - s) % NDP).wait_recv()
        first = ((z + row_offset(t)) % RX) * RX
        rows = landing[0, pl.ds(first, RX)].astype(jnp.float32).reshape(BLOCK, 256)
        tokens[0, block_rows(t), columns] = rows.astype(jnp.bfloat16)
        block_copy(t, tokens.at[0, block_rows(t), columns]).start()

    def block_ready(t):
        block_copy(t, tokens.at[0, block_rows(t), theirs]).wait_recv()

    def grad_share():
        token_local(1).wait()
        peers(lambda i: token_arrived(1, i).wait_recv())
        rows = landing[1].astype(jnp.float32).reshape(TOKENS, 256)
        tokens[1, :, columns] = rows.astype(jnp.bfloat16)
        sibling_copy(1).start()

    def x_copy(u, j):
        return pltpu.make_async_remote_copy(
            src_ref=xsend.at[u, j],
            dst_ref=xrecv.at[u, j],
            send_sem=xs_sem.at[u, j],
            recv_sem=xr_sem.at[u, j],
            device_id={"dp": x_left if j % 2 == 0 else x_right},
            device_id_type=MESH,
        )

    def b_copy(t, j):
        return pltpu.make_async_remote_copy(
            src_ref=bsend.at[t, j],
            dst_ref=brecv.at[t, j],
            send_sem=bs_sem.at[t, j],
            recv_sem=br_sem.at[t, j],
            device_id={"dp": x_left if j % 2 == 0 else x_right},
            device_id_type=MESH,
        )

    def b_send(t, j, values):
        encode(values, bsend.at[t, j])
        b_copy(t, j).start()

    def z_copy(m, j):
        return pltpu.make_async_remote_copy(
            src_ref=zsend.at[m, j],
            dst_ref=zrecv.at[m, j],
            send_sem=zs_sem.at[m, j],
            recv_sem=zr_sem.at[m, j],
            device_id={"dp": z_left if j % 2 == 0 else z_right},
            device_id_type=MESH,
        )

    def x_send(u, j, values):
        encode(values, xsend.at[u, j])
        x_copy(u, j).start()

    def z_send(m, j, values):
        encode(values, zsend.at[m, j])
        z_copy(m, j).start()

    spans = (pl.ds(0, SPAN), pl.ds(SPAN, SPAN))

    def produce(u):
        k, h, m = u // 4, (u // 2) % 2, u % 2
        back = 3 - k
        row = (z + ((back + 1) % 3 + 1) * ((back + 3) // 4)) % RX

        def partial(hop, part):
            first = (row * RX + (x + hop) % RX) * CHUNK + h * HALF
            return jnp.dot(
                tokens[m, part, :],
                weights[m, :, pl.ds(pl.multiple_of(first, HALF), HALF)],
                preferred_element_type=jnp.float32,
            )

        x_send(u, 0, partial(2, spans[0]))
        x_send(u, 1, partial(2, spans[1]))
        x_send(u, 2, partial(3, spans[1]))
        x_send(u, 3, partial(1, spans[0]))
        near[u, 0] = partial(3, spans[0])
        near[u, 1] = partial(1, spans[1])
        own[u, 0] = partial(0, spans[0])
        own[u, 1] = partial(0, spans[1])

    def block_place(t):
        row = (z + row_offset(t)) % RX
        return row // 2, pl.ds(pl.multiple_of((row % 2) * BLOCK, BLOCK), BLOCK)

    def produce_block(t):
        row = (z + 2) % RX

        def partial(hop, h):
            first = (row * RX + (x + hop) % RX) * CHUNK + h * HALF
            return jnp.dot(
                tokens[0, block_rows(t), :],
                weights[0, :, pl.ds(pl.multiple_of(first, HALF), HALF)],
                preferred_element_type=jnp.float32,
            )

        b_send(t, 0, partial(2, 0))
        b_send(t, 1, partial(2, 1))
        b_send(t, 2, partial(3, 1))
        b_send(t, 3, partial(1, 0))
        near_block[t, 0] = partial(3, 0)
        near_block[t, 1] = partial(1, 1)
        span, rows = block_place(t)
        own[0, span, rows, :] = partial(0, 0)
        own[2, span, rows, :] = partial(0, 1)

    def combine_block(t):
        for j in range(2):
            b_copy(t, j).wait_recv()
            b_send(t, 4 + j, near_block[t, j] + decode(brecv.at[t, j]))

    def finish_block(t):
        for j in range(2, 6):
            b_copy(t, j).wait_recv()
        span, rows = block_place(t)
        own[0, span, rows, :] += decode(brecv.at[t, 4]) + decode(brecv.at[t, 3])
        own[2, span, rows, :] += decode(brecv.at[t, 5]) + decode(brecv.at[t, 2])

        @pl.when(t == RX - 1)
        def _():
            for q in (0, 2):
                z_send(q, 0, own[q, 0])
                z_send(q, 1, own[q, 1])

    def combine(u):
        for j in range(2):
            x_copy(u, j).wait_recv()
            x_send(u, 4 + j, near[u, j] + decode(xrecv.at[u, j]))

    def finish(u):
        k, q = u // 4, u % 4
        for j in range(2, 6):
            x_copy(u, j).wait_recv()
        own[u, 0] += decode(xrecv.at[u, 4]) + decode(xrecv.at[u, 3])
        own[u, 1] += decode(xrecv.at[u, 5]) + decode(xrecv.at[u, 2])

        @pl.when(k == 0)
        def _():
            z_send(q, 0, own[u, 0])
            z_send(q, 1, own[u, 1])

        @pl.when(k == 1)
        def _():
            z_send(q, 3, own[u, 0])
            z_copy(q, 1).wait_recv()
            z_send(q, 5, own[u, 1] + decode(zrecv.at[q, 1]))

        @pl.when(k == 2)
        def _():
            z_send(q, 2, own[u, 1])
            z_copy(q, 0).wait_recv()
            z_send(q, 4, own[u, 0] + decode(zrecv.at[q, 0]))

        @pl.when(k == 3)
        def _():
            for j in range(2, 6):
                z_copy(q, j).wait_recv()
            final[q % 2, spans[0], :] = (
                own[u, 0] + decode(zrecv.at[q, 4]) + decode(zrecv.at[q, 3])
            )
            final[q % 2, spans[1], :] = (
                own[u, 1] + decode(zrecv.at[q, 5]) + decode(zrecv.at[q, 2])
            )

        @pl.when((k == 3) & (q % 2 == 1))
        def _():
            deliver(q // 2)

    def build_routing():
        peers(lambda i: table_arrived(i).wait_recv())
        values = table[...].astype(jnp.float32).reshape(TOKENS, HALF).T
        names = lax.broadcasted_iota(jnp.int32, (E, TOKENS), 0).astype(jnp.float32)
        total = jnp.zeros((E, TOKENS), jnp.float32)
        for k in range(8):
            total += jnp.where(values[k : k + 1, :] == names, values[8 + k : 9 + k, :], 0.0)
        routing[...] = total.astype(jnp.bfloat16)

    def out_copy(h, i):
        d = (me + i) % NDP
        return pltpu.make_async_remote_copy(
            src_ref=credit.at[h, pl.ds(pl.multiple_of(d * 16, 16), 16), :],
            dst_ref=out.at[:, pl.ds(pl.multiple_of(me * CHUNK + h * HALF, HALF), HALF)],
            send_sem=out_send.at[h, i],
            recv_sem=out_recv.at[h, i],
            device_id={"dp": d},
            device_id_type=MESH,
        )

    def out_arrived(h, i):
        s = (me + NDP - i) % NDP
        part = out.at[:, pl.ds(pl.multiple_of(s * CHUNK + h * HALF, HALF), HALF)]
        return pltpu.make_async_remote_copy(
            src_ref=part,
            dst_ref=part,
            send_sem=out_send.at[h, i],
            recv_sem=out_recv.at[h, i],
            device_id={"dp": s},
            device_id_type=MESH,
        )

    def deliver(h):
        mine = pl.ds(pl.multiple_of(me * CHUNK + h * HALF, HALF), HALF)
        score = jnp.maximum(final[0] + bias[:, mine], 0.0) * final[1]
        high = score.astype(jnp.bfloat16)
        low = (score - high.astype(jnp.float32)).astype(jnp.bfloat16)
        credit[h] = jnp.dot(
            routing[...], high, preferred_element_type=jnp.float32
        ) + jnp.dot(routing[...], low, preferred_element_type=jnp.float32)
        peers(lambda i: out_copy(h, i).start())
        out[:, mine] = credit[h, pl.ds(pl.multiple_of(me * 16, 16), 16), :]

    def unit(s):
        n = s - RX
        return n + 1 + (n + 13) // 14

    last = RX + UNITS - 2
    block_share(0)
    for m in range(2):
        weight_copy(m).wait()

    def step(s, carry):
        @pl.when(s < RX)
        def _():
            block_ready(s)
            produce_block(s)

        @pl.when(s == RX)
        def _():
            sibling_arrived(1).wait_recv()

        @pl.when((s >= RX) & (s < last))
        def _():
            produce(unit(s))

        @pl.when(s < RX - 1)
        def _():
            block_share(s + 1)

        @pl.when(s == RX + 1)
        def _():
            table_local.wait()
            peers(lambda i: table_copy(i).start())

        @pl.when(s == RX + 4)
        def _():
            build_routing()

        @pl.when((s >= 1) & (s < RX + 1))
        def _():
            combine_block(s - 1)

        @pl.when((s >= RX + 1) & (s < last + 1))
        def _():
            combine(unit(s - 1))

        @pl.when((s >= 2) & (s < RX + 2))
        def _():
            finish_block(s - 2)

        @pl.when(s >= RX + 2)
        def _():
            finish(unit(s - 2))

        @pl.when(s == RX - 1)
        def _():
            grad_share()

        return carry

    lax.fori_loop(0, last + 2, step, 0)

    for m in range(2):
        peers(lambda i, m=m: token_copy(m, i).wait_send())
    sibling_copy(1).wait_send()
    peers(lambda i: table_copy(i).wait_send())

    def x_sent(u, carry):
        for j in range(6):
            x_copy(u, j).wait_send()
        return carry

    def z_sent(m, carry):
        for j in range(6):
            z_copy(m, j).wait_send()
        return carry

    def b_sent(t, carry):
        block_copy(t, tokens.at[0, block_rows(t), columns]).wait_send()
        for j in range(6):
            b_copy(t, j).wait_send()
        return carry

    lax.fori_loop(0, RX, b_sent, 0)
    lax.fori_loop(RX, last, lambda s, carry: x_sent(unit(s), carry), 0)
    lax.fori_loop(0, 4, z_sent, 0)
    for h in range(2):
        peers(lambda i, h=h: out_arrived(h, i).wait_recv())
        peers(lambda i, h=h: out_copy(h, i).wait_send())


def on_device(
    residual, cotangent, encoder_weight, encoder_bias, decoder_weight, route_experts, route_buckets
):
    features = encoder_bias.shape[0]
    vmem = pl.BlockSpec(memory_space=pltpu.VMEM)
    hbm = pl.BlockSpec(memory_space=pltpu.HBM)
    dma = pltpu.SemaphoreType.DMA
    return pl.pallas_call(
        kernel,
        out_shape=jax.ShapeDtypeStruct((E // NDP, features), jnp.float32),
        in_specs=[hbm] * 7,
        out_specs=vmem,
        scratch_shapes=[
            pltpu.VMEM((2, WIDE, features), jnp.bfloat16),
            pltpu.VMEM((2, NDP, OWN, 256), jnp.bfloat16),
            pltpu.VMEM((2, TOKENS, WIDE), jnp.bfloat16),
            pltpu.VMEM((NDP, OWN, HALF), jnp.bfloat16),
            pltpu.VMEM((1, features), jnp.float32),
            pltpu.VMEM((8, OWN), jnp.int32),
            pltpu.VMEM((8, OWN), jnp.int32),
            pltpu.VMEM((OWN, HALF), jnp.bfloat16),
            pltpu.VMEM((UNITS, 2, SPAN, HALF), jnp.float32),
            pltpu.VMEM((RX, 2, BLOCK, HALF), jnp.float32),
            pltpu.VMEM((UNITS, 2, SPAN, HALF), jnp.float32),
            pltpu.VMEM((2, TOKENS, HALF), jnp.float32),
            pltpu.VMEM((RX, 6, BLOCK + 8, HALF), jnp.int16),
            pltpu.VMEM((RX, 6, BLOCK + 8, HALF), jnp.int16),
            pltpu.VMEM((UNITS, 6, ROWS, HALF), jnp.int16),
            pltpu.VMEM((UNITS, 6, ROWS, HALF), jnp.int16),
            pltpu.VMEM((4, 6, ROWS, HALF), jnp.int16),
            pltpu.VMEM((4, 6, ROWS, HALF), jnp.int16),
            pltpu.VMEM((2, E, HALF), jnp.float32),
            pltpu.VMEM((E, TOKENS), jnp.bfloat16),
            dma((2,)),
            dma((6,)),
            dma((2, NDP)),
            dma((2, NDP)),
            dma((2,)),
            dma((2,)),
            dma((RX,)),
            dma((RX,)),
            dma((NDP,)),
            dma((NDP,)),
            dma((RX, 6)),
            dma((RX, 6)),
            dma((UNITS, 6)),
            dma((UNITS, 6)),
            dma((4, 6)),
            dma((4, 6)),
            dma((2, NDP)),
            dma((2, NDP)),
        ],
        compiler_params=pltpu.CompilerParams(
            collective_id=0, has_side_effects=True, vmem_limit_bytes=56 * 1024 * 1024
        ),
        name="credit",
    )(
        residual,
        cotangent,
        encoder_weight,
        decoder_weight.T,
        encoder_bias.reshape(1, features),
        route_experts.T,
        route_buckets.T,
    )


def solution(mesh):
    placed = (
        P("dp", None),
        P("dp", None),
        P("dp", "feat"),
        P("feat"),
        P("feat", "dp"),
        P("dp", None),
        P("dp", None),
    )
    return jax.shard_map(
        on_device, mesh=mesh, in_specs=placed, out_specs=P("dp", "feat"), check_vma=False
    )
```

```python
import functools

import jax
import jax.numpy as jnp
from jax import lax
from jax.experimental import pallas as pl
from jax.experimental.pallas import tpu as pltpu
from jax.sharding import PartitionSpec as P

TOKENS = 384
E = 256
RX = 4
NDP = 16
OWN = TOKENS // NDP
WIDE = 512
LIVE = 448
CHUNK = 256
HALF = 128
LC, LF = 1, 2
SPAN = TOKENS // 2
ROWS = SPAN + 8
UNITS = 16
BLOCK = TOKENS // RX
MESH = pl.DeviceIdType.MESH


def code(values):
    top = jnp.max(jnp.abs(values), axis=0, keepdims=True)
    step = jnp.ceil(jnp.log(jnp.maximum(top, 1e-30)) * 32.0)
    inverse = jnp.exp(step * (-1.0 / 32.0)) * 32000.0
    codes = jnp.round(values * inverse).astype(jnp.int32).astype(jnp.int16)
    steps = jnp.broadcast_to(step, (8, values.shape[1])).astype(jnp.int32).astype(jnp.int16)
    return codes, steps


def encode(values, ref):
    count = values.shape[0]
    ref[0:count, :], ref[count : count + 8, :] = code(values)


def encode_columns(values, first, second):
    count = values.shape[0]
    codes, steps = code(values)
    for n, ref in enumerate((first, second)):
        ref[0:count, :] = codes[:, n * HALF : (n + 1) * HALF]
        ref[count : count + 8, :] = steps[:, n * HALF : (n + 1) * HALF]


def encode_rows(values, first, second):
    count = values.shape[0] // 2
    codes, steps = code(values)
    for n, ref in enumerate((first, second)):
        ref[0:count, :] = codes[n * count : (n + 1) * count, :]
        ref[count : count + 8, :] = steps


def decode(ref):
    count = ref.shape[0] - 8
    step = ref[count : count + 8, :].astype(jnp.int32).astype(jnp.float32)[0:1, :]
    scale = jnp.exp(step * (1.0 / 32.0)) * (1.0 / 32000.0)
    return ref[0:count, :].astype(jnp.int32).astype(jnp.float32) * scale


def window_start(d):
    return 896 * (d // 2) + 384 * (d % 2)


def kernel(
    residual,
    cotangent,
    encoder,
    decoder,
    bias_hbm,
    experts_hbm,
    buckets_hbm,
    out,
    weights,
    landing,
    first,
    tokens,
    table,
    bias,
    experts,
    buckets,
    codes,
    near,
    near_block,
    own,
    active,
    bsend,
    brecv,
    xsend,
    xrecv,
    zsend,
    zrecv,
    credit,
    routing,
    w_sem,
    l_sem,
    tok_send,
    tok_recv,
    near_send,
    near_recv,
    sib_send,
    sib_recv,
    sibb_send,
    sibb_recv,
    tab_send,
    tab_recv,
    bs_sem,
    br_sem,
    xs_sem,
    xr_sem,
    zs_sem,
    zr_sem,
    out_send,
    out_recv,
    out_sem,
):
    me = lax.axis_index("dp")
    feat = lax.axis_index("feat")
    core = feat % 2
    sibling = feat + 1 - 2 * core
    x = me % RX
    z = me // RX
    off = 64 * (me % 2)

    x_left = z * RX + (x + 3) % RX
    x_right = z * RX + (x + 1) % RX
    z_left = ((z + 3) % RX) * RX + x
    z_right = ((z + 1) % RX) * RX + x

    def weight_copy(m):
        source = encoder if m == 0 else decoder
        return pltpu.make_async_copy(
            source, weights.at[m, pl.ds(pl.multiple_of(off, 64), LIVE), :], w_sem.at[m]
        )

    for m in range(2):
        weight_copy(m).start()

    columns = pl.ds(pl.multiple_of(core * 256, 256), 256)

    def token_source(m, d):
        source = residual if m == 0 else cotangent
        return source.at[:, pl.ds(pl.multiple_of(window_start(d) + core * 256, 128), 256)]

    def token_local(m):
        return pltpu.make_async_copy(token_source(m, me), landing.at[m, me], l_sem.at[m])

    def first_local():
        return pltpu.make_async_copy(
            residual.at[:, pl.ds(pl.multiple_of(window_start(me), 128), WIDE)],
            first.at[x],
            l_sem.at[0],
        )

    small = [
        pltpu.make_async_copy(source, target, l_sem.at[3 + n])
        for n, (source, target) in enumerate(
            ((bias_hbm, bias), (experts_hbm, experts), (buckets_hbm, buckets))
        )
    ]
    first_local().start()
    token_local(1).start()
    for copy in small:
        copy.start()

    barrier = pltpu.get_barrier_semaphore()

    def greet(i, carry):
        pl.semaphore_signal(
            barrier, inc=1, device_id={"dp": (me + i) % NDP}, device_id_type=MESH
        )
        return carry

    lax.fori_loop(1, NDP, greet, 0)
    pl.semaphore_signal(barrier, inc=1, device_id={"feat": sibling}, device_id_type=MESH)
    pl.semaphore_wait(barrier, NDP)

    def token_copy(m, i):
        d = (me + i) % NDP
        return pltpu.make_async_remote_copy(
            src_ref=token_source(m, d),
            dst_ref=landing.at[m, me],
            send_sem=tok_send.at[m, i],
            recv_sem=tok_recv.at[m, i],
            device_id={"dp": d},
            device_id_type=MESH,
        )

    def near_source(d):
        return residual.at[:, pl.ds(pl.multiple_of(window_start(d), 128), WIDE)]

    def near_copy(hop):
        d = z * RX + (x + hop) % RX
        return pltpu.make_async_remote_copy(
            src_ref=near_source(d),
            dst_ref=first.at[x],
            send_sem=near_send.at[hop],
            recv_sem=near_recv.at[hop],
            device_id={"dp": d},
            device_id_type=MESH,
        )

    def near_arrived(hop):
        s = (x + RX - hop) % RX
        return pltpu.make_async_remote_copy(
            src_ref=first.at[s],
            dst_ref=first.at[s],
            send_sem=near_send.at[hop],
            recv_sem=near_recv.at[hop],
            device_id={"dp": z * RX + s},
            device_id_type=MESH,
        )

    def sibling_copy(m):
        part = tokens.at[m, :, columns]
        return pltpu.make_async_remote_copy(
            src_ref=part,
            dst_ref=part,
            send_sem=sib_send.at[m],
            recv_sem=sib_recv.at[m],
            device_id={"feat": sibling},
            device_id_type=MESH,
        )

    def sibling_arrived(m):
        part = tokens.at[m, :, pl.ds(pl.multiple_of(256 - core * 256, 256), 256)]
        return pltpu.make_async_remote_copy(
            src_ref=part,
            dst_ref=part,
            send_sem=sib_send.at[m],
            recv_sem=sib_recv.at[m],
            device_id={"feat": sibling},
            device_id_type=MESH,
        )

    def token_arrived(m, i):
        s = (me + NDP - i) % NDP
        part = landing.at[m, s]
        return pltpu.make_async_remote_copy(
            src_ref=part,
            dst_ref=part,
            send_sem=tok_send.at[m, i],
            recv_sem=tok_recv.at[m, i],
            device_id={"dp": s},
            device_id_type=MESH,
        )

    def table_copy(i):
        d = (me + i) % NDP
        return pltpu.make_async_remote_copy(
            src_ref=codes,
            dst_ref=table.at[me],
            send_sem=tab_send.at[i],
            recv_sem=tab_recv.at[i],
            device_id={"dp": d},
            device_id_type=MESH,
        )

    def table_arrived(i):
        s = (me + NDP - i) % NDP
        part = table.at[s]
        return pltpu.make_async_remote_copy(
            src_ref=part,
            dst_ref=part,
            send_sem=tab_send.at[i],
            recv_sem=tab_recv.at[i],
            device_id={"dp": s},
            device_id_type=MESH,
        )

    def peers(action):
        def step(i, carry):
            action(i)
            return carry

        lax.fori_loop(1, NDP, step, 0)

    def row_offset(t):
        return t + t // 2 - 2 * (t // 3)

    def place(t, hop):
        d = ((z + row_offset(t)) % RX) * RX + (x + hop) % RX
        return (d + NDP - me) % NDP

    def send_tokens(m):
        for hop in range(1, RX):
            near_copy(hop).start() if m == 0 else token_copy(m, place(0, hop)).start()

        def send_row(t, carry):
            for hop in range(RX):
                token_copy(m, place(t, hop)).start()
            return carry

        lax.fori_loop(1, RX, send_row, 0)

    send_tokens(0)
    send_tokens(1)

    blank = pl.ds(pl.multiple_of(LIVE - LIVE * (me % 2), 64), 64)
    for m in range(2):
        weights[m, blank, :] = jnp.zeros((64, weights.shape[2]), jnp.bfloat16)

    def block_rows(t):
        return pl.ds(pl.multiple_of(((z + row_offset(t)) % RX) * BLOCK, BLOCK), BLOCK)

    def block_copy(t, part):
        return pltpu.make_async_remote_copy(
            src_ref=part,
            dst_ref=part,
            send_sem=sibb_send.at[t],
            recv_sem=sibb_recv.at[t],
            device_id={"feat": sibling},
            device_id_type=MESH,
        )

    theirs = pl.ds(pl.multiple_of(256 - core * 256, 256), 256)

    def block_share(t):
        row = (z + row_offset(t)) % RX
        for hop in range(RX):
            s = row * RX + (x + hop) % RX
            token_arrived(0, (me + NDP - s) % NDP).wait_recv()
        rows = landing[0, pl.ds(row * RX, RX)].astype(jnp.float32).reshape(BLOCK, 256)
        tokens[0, block_rows(t), columns] = rows.astype(jnp.bfloat16)
        block_copy(t, tokens.at[0, block_rows(t), columns]).start()

    def first_ready():
        first_local().wait()
        for hop in range(1, RX):
            near_arrived(hop).wait_recv()
        rows = first[...].astype(jnp.float32).reshape(BLOCK, WIDE)
        tokens[0, block_rows(0), :] = rows.astype(jnp.bfloat16)

    def block_ready(t):
        block_copy(t, tokens.at[0, block_rows(t), theirs]).wait_recv()

    def grad_share():
        token_local(1).wait()
        peers(lambda i: token_arrived(1, i).wait_recv())
        rows = landing[1].astype(jnp.float32).reshape(TOKENS, 256)
        tokens[1, :, columns] = rows.astype(jnp.bfloat16)
        sibling_copy(1).start()

    def x_copy(u, j):
        return pltpu.make_async_remote_copy(
            src_ref=xsend.at[u, j],
            dst_ref=xrecv.at[u, j],
            send_sem=xs_sem.at[u, j],
            recv_sem=xr_sem.at[u, j],
            device_id={"dp": x_left if j % 2 == 0 else x_right},
            device_id_type=MESH,
        )

    def b_copy(t, j):
        return pltpu.make_async_remote_copy(
            src_ref=bsend.at[t, j],
            dst_ref=brecv.at[t, j],
            send_sem=bs_sem.at[t, j],
            recv_sem=br_sem.at[t, j],
            device_id={"dp": x_left if j % 2 == 0 else x_right},
            device_id_type=MESH,
        )

    def z_copy(m, j):
        return pltpu.make_async_remote_copy(
            src_ref=zsend.at[m, j],
            dst_ref=zrecv.at[m, j],
            send_sem=zs_sem.at[m, j],
            recv_sem=zr_sem.at[m, j],
            device_id={"dp": z_left if j % 2 == 0 else z_right},
            device_id_type=MESH,
        )

    def b_copy(t, j):
        return pltpu.make_async_remote_copy(
            src_ref=bsend.at[t, j],
            dst_ref=brecv.at[t, j],
            send_sem=bs_sem.at[t, j],
            recv_sem=br_sem.at[t, j],
            device_id={"dp": x_left if j % 2 == 0 else x_right},
            device_id_type=MESH,
        )

    def b_send(t, j, values):
        encode(values, bsend.at[t, j])
        b_copy(t, j).start()

    def z_copy(m, j):
        return pltpu.make_async_remote_copy(
            src_ref=zsend.at[m, j],
            dst_ref=zrecv.at[m, j],
            send_sem=zs_sem.at[m, j],
            recv_sem=zr_sem.at[m, j],
            device_id={"dp": z_left if j % 2 == 0 else z_right},
            device_id_type=MESH,
        )

    def x_send(u, j, values):
        encode(values, xsend.at[u, j])
        x_copy(u, j).start()

    def z_send(m, j, values):
        encode(values, zsend.at[m, j])
        z_copy(m, j).start()

    spans = (pl.ds(0, SPAN), pl.ds(SPAN, SPAN))

    def produce(u):
        k, h, m = u // 4, (u // 2) % 2, u % 2
        back = 3 - k
        row = (z + ((back + 1) % 3 + 1) * ((back + 3) // 4)) % RX

        def partial(hop):
            first = (row * RX + (x + hop) % RX) * CHUNK + h * HALF
            return jnp.dot(
                tokens[m],
                weights[m, :, pl.ds(pl.multiple_of(first, HALF), HALF)],
                preferred_element_type=jnp.float32,
            )

        encode_rows(partial(2), xsend.at[u, 0], xsend.at[u, 1])
        x_copy(u, 0).start()
        x_copy(u, 1).start()
        left, right = partial(3), partial(1)
        encode_columns(
            jnp.concatenate([left[SPAN:], right[:SPAN]], axis=1), xsend.at[u, 2], xsend.at[u, 3]
        )
        x_copy(u, 2).start()
        x_copy(u, 3).start()
        near[u, 0] = left[:SPAN]
        near[u, 1] = right[SPAN:]
        mine = partial(0)
        own[u, 0] = mine[:SPAN]
        own[u, 1] = mine[SPAN:]

    def block_place(t):
        row = (z + row_offset(t)) % RX
        return row // 2, pl.ds(pl.multiple_of((row % 2) * BLOCK, BLOCK), BLOCK)

    def produce_block(t):
        row = (z + 2) % RX

        def partial(hop):
            first = (row * RX + (x + hop) % RX) * CHUNK
            return jnp.dot(
                tokens[0, block_rows(t), :],
                weights[0, :, pl.ds(pl.multiple_of(first, CHUNK), CHUNK)],
                preferred_element_type=jnp.float32,
            )

        encode_columns(partial(2), bsend.at[t, 0], bsend.at[t, 1])
        b_copy(t, 0).start()
        b_copy(t, 1).start()
        left, right = partial(3), partial(1)
        encode_columns(
            jnp.concatenate([left[:, HALF:], right[:, :HALF]], axis=1),
            bsend.at[t, 2],
            bsend.at[t, 3],
        )
        b_copy(t, 2).start()
        b_copy(t, 3).start()
        near_block[t, 0] = left[:, :HALF]
        near_block[t, 1] = right[:, HALF:]
        mine = partial(0)
        span, rows = block_place(t)
        own[0, span, rows, :] = mine[:, :HALF]
        own[2, span, rows, :] = mine[:, HALF:]

    def combine_block(t):
        for j in range(2):
            b_copy(t, j).wait_recv()
        encode_columns(
            jnp.concatenate(
                [near_block[t, j] + decode(brecv.at[t, j]) for j in range(2)], axis=1
            ),
            bsend.at[t, 4],
            bsend.at[t, 5],
        )
        b_copy(t, 4).start()
        b_copy(t, 5).start()

    def finish_block(t):
        for j in range(2, 6):
            b_copy(t, j).wait_recv()
        span, rows = block_place(t)
        own[0, span, rows, :] += decode(brecv.at[t, 4]) + decode(brecv.at[t, 3])
        own[2, span, rows, :] += decode(brecv.at[t, 5]) + decode(brecv.at[t, 2])

        @pl.when(t == RX - 1)
        def _():
            for q in (0, 2):
                z_send(q, 0, own[q, 0])
                z_send(q, 1, own[q, 1])

    def combine(u):
        for j in range(2):
            x_copy(u, j).wait_recv()
        encode_columns(
            jnp.concatenate([near[u, j] + decode(xrecv.at[u, j]) for j in range(2)], axis=1),
            xsend.at[u, 4],
            xsend.at[u, 5],
        )
        x_copy(u, 4).start()
        x_copy(u, 5).start()

    def finish(u):
        k, q = u // 4, u % 4
        for j in range(2, 4):
            x_copy(u, j).wait_recv()
        own[u, 0] += decode(xrecv.at[u, 3])
        own[u, 1] += decode(xrecv.at[u, 2])

        @pl.when(k == 3)
        def _():
            for j in range(2, 6):
                z_copy(q, j).wait_recv()
            own[u, 0] += decode(zrecv.at[q, 4]) + decode(zrecv.at[q, 3])
            own[u, 1] += decode(zrecv.at[q, 5]) + decode(zrecv.at[q, 2])

        for j in range(4, 6):
            x_copy(u, j).wait_recv()
        own[u, 0] += decode(xrecv.at[u, 4])
        own[u, 1] += decode(xrecv.at[u, 5])

        @pl.when(k == 0)
        def _():
            z_send(q, 0, own[u, 0])
            z_send(q, 1, own[u, 1])

        @pl.when(k == 1)
        def _():
            z_send(q, 3, own[u, 0])
            z_copy(q, 1).wait_recv()
            z_send(q, 5, own[u, 1] + decode(zrecv.at[q, 1]))

        @pl.when(k == 2)
        def _():
            z_send(q, 2, own[u, 1])
            z_copy(q, 0).wait_recv()
            z_send(q, 4, own[u, 0] + decode(zrecv.at[q, 0]))

        @pl.when((k == 3) & (q % 2 == 0))
        def _():
            mine = pl.ds(pl.multiple_of(me * CHUNK + (q // 2) * HALF, HALF), HALF)
            for n in range(2):
                active[spans[n], :] = jnp.maximum(own[u, n] + bias[:, mine], 0.0)

        @pl.when((k == 3) & (q % 2 == 1))
        def _():
            deliver(u, q // 2)

    def build_routing():
        peers(lambda i: table_arrived(i).wait_recv())
        values = table[...].astype(jnp.float32).reshape(TOKENS, HALF).T
        names = lax.broadcasted_iota(jnp.int32, (E, TOKENS), 0).astype(jnp.float32)
        total = jnp.zeros((E, TOKENS), jnp.float32)
        for k in range(8):
            total += jnp.where(values[k : k + 1, :] == names, values[8 + k : 9 + k, :], 0.0)
        routing[...] = total.astype(jnp.bfloat16)

    def out_copy(h, i):
        d = (me + i) % NDP
        return pltpu.make_async_remote_copy(
            src_ref=credit.at[h, pl.ds(pl.multiple_of(d * 16, 16), 16), :],
            dst_ref=out.at[:, pl.ds(pl.multiple_of(me * CHUNK + h * HALF, HALF), HALF)],
            send_sem=out_send.at[h, i],
            recv_sem=out_recv.at[h, i],
            device_id={"dp": d},
            device_id_type=MESH,
        )

    def out_local(h):
        return pltpu.make_async_copy(
            credit.at[h, pl.ds(pl.multiple_of(me * 16, 16), 16), :],
            out.at[:, pl.ds(pl.multiple_of(me * CHUNK + h * HALF, HALF), HALF)],
            out_sem.at[h],
        )

    def out_arrived(h, i):
        s = (me + NDP - i) % NDP
        part = out.at[:, pl.ds(pl.multiple_of(s * CHUNK + h * HALF, HALF), HALF)]
        return pltpu.make_async_remote_copy(
            src_ref=part,
            dst_ref=part,
            send_sem=out_send.at[h, i],
            recv_sem=out_recv.at[h, i],
            device_id={"dp": s},
            device_id_type=MESH,
        )

    def deliver(u, h):
        mine = pl.ds(pl.multiple_of(me * CHUNK + h * HALF, HALF), HALF)
        score = active[...] * jnp.concatenate([own[u, 0], own[u, 1]], axis=0)
        high = score.astype(jnp.bfloat16)
        low = (score - high.astype(jnp.float32)).astype(jnp.bfloat16)
        credit[h] = jnp.dot(
            routing[...], high, preferred_element_type=jnp.float32
        ) + jnp.dot(routing[...], low, preferred_element_type=jnp.float32)
        for t in (3, 1, 2, 0):
            for hop in range(RX):
                if t + hop > 0:
                    out_copy(h, place(t, hop)).start()
        out_local(h).start()

    def unit(s):
        n = s - RX
        return n + 1 + (n + 13) // 14

    last = RX + UNITS - 2
    for m in range(2):
        weight_copy(m).wait()
    first_ready()

    table_local = pltpu.make_async_copy(codes, table.at[me], l_sem.at[2])

    def build_codes():
        for copy in small:
            copy.wait()
        codes[...] = jnp.zeros_like(codes)
        named = experts[...].astype(jnp.float32)
        weight = buckets[...].astype(jnp.float32)
        both = jnp.concatenate([named, weight], axis=0).astype(jnp.bfloat16)
        same = lax.broadcasted_iota(jnp.int32, (OWN, OWN), 0) == lax.broadcasted_iota(
            jnp.int32, (OWN, OWN), 1
        )
        codes[:, 0:16] = lax.dot_general(
            jnp.where(same, 1.0, 0.0).astype(jnp.bfloat16),
            both,
            (((1,), (1,)), ((), ())),
            preferred_element_type=jnp.float32,
        ).astype(jnp.bfloat16)
        table_local.start()

    def step(s, carry):
        @pl.when(s < RX)
        def _():
            @pl.when(s > 0)
            def _():
                block_ready(s)

            produce_block(s)


        @pl.when(s == RX)
        def _():
            sibling_arrived(1).wait_recv()

        @pl.when((s >= RX) & (s < last))
        def _():
            produce(unit(s))

        @pl.when(s < RX - 1)
        def _():
            block_share(s + 1)

        @pl.when(s == RX + 1)
        def _():
            build_codes()
            table_local.wait()
            peers(lambda i: table_copy(i).start())

        @pl.when(s == RX + 4)
        def _():
            build_routing()

        @pl.when((s >= LC) & (s < RX + LC))
        def _():
            combine_block(s - LC)

        @pl.when((s >= RX + LC) & (s < last + LC))
        def _():
            combine(unit(s - LC))

        @pl.when((s >= LF) & (s < RX + LF))
        def _():
            finish_block(s - LF)

        @pl.when(s >= RX + LF)
        def _():
            finish(unit(s - LF))

        @pl.when(s == RX - 1)
        def _():
            grad_share()

        return carry

    lax.fori_loop(0, last + LF, step, 0)

    for hop in range(1, RX):
        near_copy(hop).wait_send()

    def rows_sent(t, carry):
        for hop in range(RX):
            token_copy(0, place(t, hop)).wait_send()
        return carry

    lax.fori_loop(1, RX, rows_sent, 0)
    peers(lambda i: token_copy(1, i).wait_send())
    sibling_copy(1).wait_send()
    peers(lambda i: table_copy(i).wait_send())

    def x_sent(u, carry):
        for j in range(6):
            x_copy(u, j).wait_send()
        return carry

    def z_sent(m, carry):
        for j in range(6):
            z_copy(m, j).wait_send()
        return carry

    def b_sent(t, carry):
        @pl.when(t > 0)
        def _():
            block_copy(t, tokens.at[0, block_rows(t), columns]).wait_send()

        for j in range(6):
            b_copy(t, j).wait_send()
        return carry

    lax.fori_loop(0, RX, b_sent, 0)
    lax.fori_loop(RX, last, lambda s, carry: x_sent(unit(s), carry), 0)
    lax.fori_loop(0, 4, z_sent, 0)
    for h in range(2):
        out_local(h).wait()
        peers(lambda i, h=h: out_arrived(h, i).wait_recv())
        peers(lambda i, h=h: out_copy(h, i).wait_send())


def on_device(
    residual, cotangent, encoder_weight, encoder_bias, decoder_weight, route_experts, route_buckets
):
    features = encoder_bias.shape[0]
    hbm = pl.BlockSpec(memory_space=pltpu.HBM)
    dma = pltpu.SemaphoreType.DMA
    eighths = pl.pallas_call(
        kernel,
        out_shape=jax.ShapeDtypeStruct((E // NDP, features), jnp.float32),
        in_specs=[hbm] * 7,
        out_specs=hbm,
        scratch_shapes=[
            pltpu.VMEM((2, WIDE, features), jnp.bfloat16),
            pltpu.VMEM((2, NDP, OWN, 256), jnp.bfloat16),
            pltpu.VMEM((RX, OWN, WIDE), jnp.bfloat16),
            pltpu.VMEM((2, TOKENS, WIDE), jnp.bfloat16),
            pltpu.VMEM((NDP, OWN, HALF), jnp.bfloat16),
            pltpu.VMEM((1, features), jnp.float32),
            pltpu.VMEM((8, OWN), jnp.int32),
            pltpu.VMEM((8, OWN), jnp.int32),
            pltpu.VMEM((OWN, HALF), jnp.bfloat16),
            pltpu.VMEM((UNITS, 2, SPAN, HALF), jnp.float32),
            pltpu.VMEM((RX, 2, BLOCK, HALF), jnp.float32),
            pltpu.VMEM((UNITS, 2, SPAN, HALF), jnp.float32),
            pltpu.VMEM((TOKENS, HALF), jnp.float32),
            pltpu.VMEM((RX, 6, BLOCK + 8, HALF), jnp.int16),
            pltpu.VMEM((RX, 6, BLOCK + 8, HALF), jnp.int16),
            pltpu.VMEM((UNITS, 6, ROWS, HALF), jnp.int16),
            pltpu.VMEM((UNITS, 6, ROWS, HALF), jnp.int16),
            pltpu.VMEM((4, 6, ROWS, HALF), jnp.int16),
            pltpu.VMEM((4, 6, ROWS, HALF), jnp.int16),
            pltpu.VMEM((2, E, HALF), jnp.float32),
            pltpu.VMEM((E, TOKENS), jnp.bfloat16),
            dma((2,)),
            dma((6,)),
            dma((2, NDP)),
            dma((2, NDP)),
            dma((RX,)),
            dma((RX,)),
            dma((2,)),
            dma((2,)),
            dma((RX,)),
            dma((RX,)),
            dma((NDP,)),
            dma((NDP,)),
            dma((RX, 6)),
            dma((RX, 6)),
            dma((UNITS, 6)),
            dma((UNITS, 6)),
            dma((4, 6)),
            dma((4, 6)),
            dma((2, NDP)),
            dma((2, NDP)),
            dma((2,)),
        ],
        compiler_params=pltpu.CompilerParams(
            collective_id=0, has_side_effects=True, vmem_limit_bytes=56 * 1024 * 1024
        ),
        name="credit",
    )(
        residual,
        cotangent,
        encoder_weight,
        decoder_weight.T,
        encoder_bias.reshape(1, features),
        route_experts.T,
        route_buckets.T,
    )
    return eighths * 0.125


def solution(mesh):
    placed = (
        P("dp", None),
        P("dp", None),
        P("dp", "feat"),
        P("feat"),
        P("feat", "dp"),
        P("dp", None),
        P("dp", None),
    )
    return jax.shard_map(
        on_device, mesh=mesh, in_specs=placed, out_specs=P("dp", "feat"), check_vma=False
    )
```

```python
import functools

import jax
import jax.numpy as jnp
from jax import lax
from jax.experimental import pallas as pl
from jax.experimental.pallas import tpu as pltpu
from jax.sharding import PartitionSpec as P

TOKENS = 384
E = 256
RX = 4
NDP = 16
OWN = TOKENS // NDP
WIDE = 512
LIVE = 448
CHUNK = 256
HALF = 128
LC, LF = 1, 3
SPAN = TOKENS // 2
ROWS = SPAN + 8
UNITS = 16
BLOCK = TOKENS // RX
MESH = pl.DeviceIdType.MESH


def code(values):
    top = jnp.max(jnp.abs(values), axis=0, keepdims=True)
    step = jnp.ceil(jnp.log(jnp.maximum(top, 1e-30)) * 32.0)
    inverse = jnp.exp(step * (-1.0 / 32.0)) * 32000.0
    codes = jnp.round(values * inverse).astype(jnp.int32).astype(jnp.int16)
    steps = jnp.broadcast_to(step, (8, values.shape[1])).astype(jnp.int32).astype(jnp.int16)
    return codes, steps


def encode(values, ref):
    count = values.shape[0]
    ref[0:count, :], ref[count : count + 8, :] = code(values)


def encode_columns(values, first, second):
    count = values.shape[0]
    codes, steps = code(values)
    for n, ref in enumerate((first, second)):
        ref[0:count, :] = codes[:, n * HALF : (n + 1) * HALF]
        ref[count : count + 8, :] = steps[:, n * HALF : (n + 1) * HALF]


def encode_rows(values, first, second):
    count = values.shape[0] // 2
    codes, steps = code(values)
    for n, ref in enumerate((first, second)):
        ref[0:count, :] = codes[n * count : (n + 1) * count, :]
        ref[count : count + 8, :] = steps


def decode(ref):
    count = ref.shape[0] - 8
    step = ref[count : count + 8, :].astype(jnp.int32).astype(jnp.float32)[0:1, :]
    scale = jnp.exp(step * (1.0 / 32.0)) * (1.0 / 32000.0)
    return ref[0:count, :].astype(jnp.int32).astype(jnp.float32) * scale


def window_start(d):
    return 896 * (d // 2) + 384 * (d % 2)


def kernel(
    residual,
    cotangent,
    encoder,
    decoder,
    bias_hbm,
    experts_hbm,
    buckets_hbm,
    out,
    weights,
    landing,
    first,
    tokens,
    table,
    bias,
    experts,
    buckets,
    codes,
    near,
    near_block,
    own,
    active,
    bsend,
    brecv,
    xsend,
    xrecv,
    zsend,
    zrecv,
    credit,
    routing,
    w_sem,
    l_sem,
    tok_send,
    tok_recv,
    near_send,
    near_recv,
    sib_send,
    sib_recv,
    sibb_send,
    sibb_recv,
    tab_send,
    tab_recv,
    bs_sem,
    br_sem,
    xs_sem,
    xr_sem,
    zs_sem,
    zr_sem,
    out_send,
    out_recv,
    out_sem,
):
    me = lax.axis_index("dp")
    feat = lax.axis_index("feat")
    core = feat % 2
    sibling = feat + 1 - 2 * core
    x = me % RX
    z = me // RX
    off = 64 * (me % 2)

    x_left = z * RX + (x + 3) % RX
    x_right = z * RX + (x + 1) % RX
    z_left = ((z + 3) % RX) * RX + x
    z_right = ((z + 1) % RX) * RX + x

    def weight_copy(m):
        source = encoder if m == 0 else decoder
        return pltpu.make_async_copy(
            source, weights.at[m, pl.ds(pl.multiple_of(off, 64), LIVE), :], w_sem.at[m]
        )

    for m in range(2):
        weight_copy(m).start()

    columns = pl.ds(pl.multiple_of(core * 256, 256), 256)

    def token_source(m, d):
        source = residual if m == 0 else cotangent
        return source.at[:, pl.ds(pl.multiple_of(window_start(d) + core * 256, 128), 256)]

    def token_local(m):
        return pltpu.make_async_copy(token_source(m, me), landing.at[m, me], l_sem.at[m])

    def first_local():
        return pltpu.make_async_copy(
            residual.at[:, pl.ds(pl.multiple_of(window_start(me), 128), WIDE)],
            first.at[x],
            l_sem.at[0],
        )

    small = [
        pltpu.make_async_copy(source, target, l_sem.at[3 + n])
        for n, (source, target) in enumerate(
            ((bias_hbm, bias), (experts_hbm, experts), (buckets_hbm, buckets))
        )
    ]
    first_local().start()
    token_local(1).start()
    for copy in small:
        copy.start()

    barrier = pltpu.get_barrier_semaphore()

    def greet(i, carry):
        pl.semaphore_signal(
            barrier, inc=1, device_id={"dp": (me + i) % NDP}, device_id_type=MESH
        )
        return carry

    lax.fori_loop(1, NDP, greet, 0)
    pl.semaphore_signal(barrier, inc=1, device_id={"feat": sibling}, device_id_type=MESH)
    pl.semaphore_wait(barrier, NDP)

    def token_copy(m, i):
        d = (me + i) % NDP
        return pltpu.make_async_remote_copy(
            src_ref=token_source(m, d),
            dst_ref=landing.at[m, me],
            send_sem=tok_send.at[m, i],
            recv_sem=tok_recv.at[m, i],
            device_id={"dp": d},
            device_id_type=MESH,
        )

    def near_source(d):
        return residual.at[:, pl.ds(pl.multiple_of(window_start(d), 128), WIDE)]

    def near_copy(hop):
        d = z * RX + (x + hop) % RX
        return pltpu.make_async_remote_copy(
            src_ref=near_source(d),
            dst_ref=first.at[x],
            send_sem=near_send.at[hop],
            recv_sem=near_recv.at[hop],
            device_id={"dp": d},
            device_id_type=MESH,
        )

    def near_arrived(hop):
        s = (x + RX - hop) % RX
        return pltpu.make_async_remote_copy(
            src_ref=first.at[s],
            dst_ref=first.at[s],
            send_sem=near_send.at[hop],
            recv_sem=near_recv.at[hop],
            device_id={"dp": z * RX + s},
            device_id_type=MESH,
        )

    def sibling_copy(m):
        part = tokens.at[m, :, columns]
        return pltpu.make_async_remote_copy(
            src_ref=part,
            dst_ref=part,
            send_sem=sib_send.at[m],
            recv_sem=sib_recv.at[m],
            device_id={"feat": sibling},
            device_id_type=MESH,
        )

    def sibling_arrived(m):
        part = tokens.at[m, :, pl.ds(pl.multiple_of(256 - core * 256, 256), 256)]
        return pltpu.make_async_remote_copy(
            src_ref=part,
            dst_ref=part,
            send_sem=sib_send.at[m],
            recv_sem=sib_recv.at[m],
            device_id={"feat": sibling},
            device_id_type=MESH,
        )

    def token_arrived(m, i):
        s = (me + NDP - i) % NDP
        part = landing.at[m, s]
        return pltpu.make_async_remote_copy(
            src_ref=part,
            dst_ref=part,
            send_sem=tok_send.at[m, i],
            recv_sem=tok_recv.at[m, i],
            device_id={"dp": s},
            device_id_type=MESH,
        )

    def table_copy(i):
        d = (me + i) % NDP
        return pltpu.make_async_remote_copy(
            src_ref=codes,
            dst_ref=table.at[me],
            send_sem=tab_send.at[i],
            recv_sem=tab_recv.at[i],
            device_id={"dp": d},
            device_id_type=MESH,
        )

    def table_arrived(i):
        s = (me + NDP - i) % NDP
        part = table.at[s]
        return pltpu.make_async_remote_copy(
            src_ref=part,
            dst_ref=part,
            send_sem=tab_send.at[i],
            recv_sem=tab_recv.at[i],
            device_id={"dp": s},
            device_id_type=MESH,
        )

    def peers(action):
        def step(i, carry):
            action(i)
            return carry

        lax.fori_loop(1, NDP, step, 0)

    def row_offset(t):
        return t + t // 2 - 2 * (t // 3)

    def place(t, hop):
        d = ((z + row_offset(t)) % RX) * RX + (x + hop) % RX
        return (d + NDP - me) % NDP

    def send_tokens(m):
        for hop in range(1, RX):
            near_copy(hop).start() if m == 0 else token_copy(m, place(0, hop)).start()

        def send_row(t, carry):
            for hop in range(RX):
                token_copy(m, place(t, hop)).start()
            return carry

        lax.fori_loop(1, RX, send_row, 0)

    send_tokens(0)
    send_tokens(1)

    blank = pl.ds(pl.multiple_of(LIVE - LIVE * (me % 2), 64), 64)
    for m in range(2):
        weights[m, blank, :] = jnp.zeros((64, weights.shape[2]), jnp.bfloat16)

    def block_rows(t):
        return pl.ds(pl.multiple_of(((z + row_offset(t)) % RX) * BLOCK, BLOCK), BLOCK)

    def block_copy(t, part):
        return pltpu.make_async_remote_copy(
            src_ref=part,
            dst_ref=part,
            send_sem=sibb_send.at[t],
            recv_sem=sibb_recv.at[t],
            device_id={"feat": sibling},
            device_id_type=MESH,
        )

    theirs = pl.ds(pl.multiple_of(256 - core * 256, 256), 256)

    def block_share(t):
        row = (z + row_offset(t)) % RX
        for hop in range(RX):
            s = row * RX + (x + hop) % RX
            token_arrived(0, (me + NDP - s) % NDP).wait_recv()
        rows = landing[0, pl.ds(row * RX, RX)].astype(jnp.float32).reshape(BLOCK, 256)
        tokens[0, block_rows(t), columns] = rows.astype(jnp.bfloat16)
        block_copy(t, tokens.at[0, block_rows(t), columns]).start()

    def first_ready():
        first_local().wait()
        for hop in range(1, RX):
            near_arrived(hop).wait_recv()
        rows = first[...].astype(jnp.float32).reshape(BLOCK, WIDE)
        tokens[0, block_rows(0), :] = rows.astype(jnp.bfloat16)

    def block_ready(t):
        block_copy(t, tokens.at[0, block_rows(t), theirs]).wait_recv()

    def grad_share():
        token_local(1).wait()
        peers(lambda i: token_arrived(1, i).wait_recv())
        rows = landing[1].astype(jnp.float32).reshape(TOKENS, 256)
        tokens[1, :, columns] = rows.astype(jnp.bfloat16)
        sibling_copy(1).start()

    def x_copy(u, j):
        return pltpu.make_async_remote_copy(
            src_ref=xsend.at[u, j],
            dst_ref=xrecv.at[u, j],
            send_sem=xs_sem.at[u, j],
            recv_sem=xr_sem.at[u, j],
            device_id={"dp": x_left if j % 2 == 0 else x_right},
            device_id_type=MESH,
        )

    def b_copy(t, j):
        return pltpu.make_async_remote_copy(
            src_ref=bsend.at[t, j],
            dst_ref=brecv.at[t, j],
            send_sem=bs_sem.at[t, j],
            recv_sem=br_sem.at[t, j],
            device_id={"dp": x_left if j % 2 == 0 else x_right},
            device_id_type=MESH,
        )

    def z_copy(m, j):
        return pltpu.make_async_remote_copy(
            src_ref=zsend.at[m, j],
            dst_ref=zrecv.at[m, j],
            send_sem=zs_sem.at[m, j],
            recv_sem=zr_sem.at[m, j],
            device_id={"dp": z_left if j % 2 == 0 else z_right},
            device_id_type=MESH,
        )

    def b_copy(t, j):
        return pltpu.make_async_remote_copy(
            src_ref=bsend.at[t, j],
            dst_ref=brecv.at[t, j],
            send_sem=bs_sem.at[t, j],
            recv_sem=br_sem.at[t, j],
            device_id={"dp": x_left if j % 2 == 0 else x_right},
            device_id_type=MESH,
        )

    def b_send(t, j, values):
        encode(values, bsend.at[t, j])
        b_copy(t, j).start()

    def z_copy(m, j):
        return pltpu.make_async_remote_copy(
            src_ref=zsend.at[m, j],
            dst_ref=zrecv.at[m, j],
            send_sem=zs_sem.at[m, j],
            recv_sem=zr_sem.at[m, j],
            device_id={"dp": z_left if j % 2 == 0 else z_right},
            device_id_type=MESH,
        )

    def x_send(u, j, values):
        encode(values, xsend.at[u, j])
        x_copy(u, j).start()

    def z_send(m, j, values):
        encode(values, zsend.at[m, j])
        z_copy(m, j).start()

    spans = (pl.ds(0, SPAN), pl.ds(SPAN, SPAN))

    def produce(u):
        k, h, m = u // 4, (u // 2) % 2, u % 2
        back = 3 - k
        row = (z + ((back + 1) % 3 + 1) * ((back + 3) // 4)) % RX

        def partial(hop):
            first = (row * RX + (x + hop) % RX) * CHUNK + h * HALF
            return jnp.dot(
                tokens[m],
                weights[m, :, pl.ds(pl.multiple_of(first, HALF), HALF)],
                preferred_element_type=jnp.float32,
            )

        encode_rows(partial(2), xsend.at[u, 0], xsend.at[u, 1])
        x_copy(u, 0).start()
        x_copy(u, 1).start()
        left, right = partial(3), partial(1)
        encode_columns(
            jnp.concatenate([left[SPAN:], right[:SPAN]], axis=1), xsend.at[u, 2], xsend.at[u, 3]
        )
        x_copy(u, 2).start()
        x_copy(u, 3).start()
        near[u, 0] = left[:SPAN]
        near[u, 1] = right[SPAN:]
        mine = partial(0)
        own[u, 0] = mine[:SPAN]
        own[u, 1] = mine[SPAN:]

    def block_place(t):
        row = (z + row_offset(t)) % RX
        return row // 2, pl.ds(pl.multiple_of((row % 2) * BLOCK, BLOCK), BLOCK)

    def produce_block(t):
        row = (z + 2) % RX

        def partial(hop):
            first = (row * RX + (x + hop) % RX) * CHUNK
            return jnp.dot(
                tokens[0, block_rows(t), :],
                weights[0, :, pl.ds(pl.multiple_of(first, CHUNK), CHUNK)],
                preferred_element_type=jnp.float32,
            )

        encode_columns(partial(2), bsend.at[t, 0], bsend.at[t, 1])
        b_copy(t, 0).start()
        b_copy(t, 1).start()
        left, right = partial(3), partial(1)
        encode_columns(
            jnp.concatenate([left[:, HALF:], right[:, :HALF]], axis=1),
            bsend.at[t, 2],
            bsend.at[t, 3],
        )
        b_copy(t, 2).start()
        b_copy(t, 3).start()
        near_block[t, 0] = left[:, :HALF]
        near_block[t, 1] = right[:, HALF:]
        mine = partial(0)
        span, rows = block_place(t)
        own[0, span, rows, :] = mine[:, :HALF]
        own[2, span, rows, :] = mine[:, HALF:]

    def combine_block(t):
        for j in range(2):
            b_copy(t, j).wait_recv()
        encode_columns(
            jnp.concatenate(
                [near_block[t, j] + decode(brecv.at[t, j]) for j in range(2)], axis=1
            ),
            bsend.at[t, 4],
            bsend.at[t, 5],
        )
        b_copy(t, 4).start()
        b_copy(t, 5).start()

    def finish_block(t):
        for j in range(2, 6):
            b_copy(t, j).wait_recv()
        span, rows = block_place(t)
        own[0, span, rows, :] += decode(brecv.at[t, 4]) + decode(brecv.at[t, 3])
        own[2, span, rows, :] += decode(brecv.at[t, 5]) + decode(brecv.at[t, 2])

        @pl.when(t == RX - 1)
        def _():
            for q in (0, 2):
                z_send(q, 0, own[q, 0])
                z_send(q, 1, own[q, 1])

    def combine(u):
        for j in range(2):
            x_copy(u, j).wait_recv()
        encode_columns(
            jnp.concatenate([near[u, j] + decode(xrecv.at[u, j]) for j in range(2)], axis=1),
            xsend.at[u, 4],
            xsend.at[u, 5],
        )
        x_copy(u, 4).start()
        x_copy(u, 5).start()

    def finish(u):
        k, q = u // 4, u % 4
        for j in range(2, 4):
            x_copy(u, j).wait_recv()
        own[u, 0] += decode(xrecv.at[u, 3])
        own[u, 1] += decode(xrecv.at[u, 2])

        @pl.when(k == 3)
        def _():
            for j in range(2, 6):
                z_copy(q, j).wait_recv()
            own[u, 0] += decode(zrecv.at[q, 4]) + decode(zrecv.at[q, 3])
            own[u, 1] += decode(zrecv.at[q, 5]) + decode(zrecv.at[q, 2])

        for j in range(4, 6):
            x_copy(u, j).wait_recv()
        own[u, 0] += decode(xrecv.at[u, 4])
        own[u, 1] += decode(xrecv.at[u, 5])

        @pl.when(k == 0)
        def _():
            z_send(q, 0, own[u, 0])
            z_send(q, 1, own[u, 1])

        @pl.when(k == 1)
        def _():
            z_send(q, 3, own[u, 0])
            z_copy(q, 1).wait_recv()
            z_send(q, 5, own[u, 1] + decode(zrecv.at[q, 1]))

        @pl.when(k == 2)
        def _():
            z_send(q, 2, own[u, 1])
            z_copy(q, 0).wait_recv()
            z_send(q, 4, own[u, 0] + decode(zrecv.at[q, 0]))

        @pl.when((k == 3) & (q % 2 == 0))
        def _():
            mine = pl.ds(pl.multiple_of(me * CHUNK + (q // 2) * HALF, HALF), HALF)
            for n in range(2):
                active[spans[n], :] = jnp.maximum(own[u, n] + bias[:, mine], 0.0)

        @pl.when((k == 3) & (q % 2 == 1))
        def _():
            deliver(u, q // 2)

    def build_routing():
        peers(lambda i: table_arrived(i).wait_recv())
        values = table[...].astype(jnp.float32).reshape(TOKENS, HALF).T
        names = lax.broadcasted_iota(jnp.int32, (E, TOKENS), 0).astype(jnp.float32)
        total = jnp.zeros((E, TOKENS), jnp.float32)
        for k in range(8):
            total += jnp.where(values[k : k + 1, :] == names, values[8 + k : 9 + k, :], 0.0)
        routing[...] = total.astype(jnp.bfloat16)

    def out_copy(h, i):
        d = (me + i) % NDP
        return pltpu.make_async_remote_copy(
            src_ref=credit.at[h, pl.ds(pl.multiple_of(d * 16, 16), 16), :],
            dst_ref=out.at[:, pl.ds(pl.multiple_of(me * CHUNK + h * HALF, HALF), HALF)],
            send_sem=out_send.at[h, i],
            recv_sem=out_recv.at[h, i],
            device_id={"dp": d},
            device_id_type=MESH,
        )

    def out_local(h):
        return pltpu.make_async_copy(
            credit.at[h, pl.ds(pl.multiple_of(me * 16, 16), 16), :],
            out.at[:, pl.ds(pl.multiple_of(me * CHUNK + h * HALF, HALF), HALF)],
            out_sem.at[h],
        )

    def out_arrived(h, i):
        s = (me + NDP - i) % NDP
        part = out.at[:, pl.ds(pl.multiple_of(s * CHUNK + h * HALF, HALF), HALF)]
        return pltpu.make_async_remote_copy(
            src_ref=part,
            dst_ref=part,
            send_sem=out_send.at[h, i],
            recv_sem=out_recv.at[h, i],
            device_id={"dp": s},
            device_id_type=MESH,
        )

    def deliver(u, h):
        mine = pl.ds(pl.multiple_of(me * CHUNK + h * HALF, HALF), HALF)
        score = active[...] * jnp.concatenate([own[u, 0], own[u, 1]], axis=0)
        high = score.astype(jnp.bfloat16)
        low = (score - high.astype(jnp.float32)).astype(jnp.bfloat16)
        credit[h] = jnp.dot(
            routing[...], high, preferred_element_type=jnp.float32
        ) + jnp.dot(routing[...], low, preferred_element_type=jnp.float32)
        for t in (3, 1, 2, 0):
            for hop in range(RX):
                if t + hop > 0:
                    out_copy(h, place(t, hop)).start()
        out_local(h).start()

    def unit(s):
        n = s - RX
        return n + 1 + (n + 13) // 14

    last = RX + UNITS - 2
    for m in range(2):
        weight_copy(m).wait()
    first_ready()

    table_local = pltpu.make_async_copy(codes, table.at[me], l_sem.at[2])

    def build_codes():
        for copy in small:
            copy.wait()
        codes[...] = jnp.zeros_like(codes)
        named = experts[...].astype(jnp.float32)
        weight = buckets[...].astype(jnp.float32)
        both = jnp.concatenate([named, weight], axis=0).astype(jnp.bfloat16)
        same = lax.broadcasted_iota(jnp.int32, (OWN, OWN), 0) == lax.broadcasted_iota(
            jnp.int32, (OWN, OWN), 1
        )
        codes[:, 0:16] = lax.dot_general(
            jnp.where(same, 1.0, 0.0).astype(jnp.bfloat16),
            both,
            (((1,), (1,)), ((), ())),
            preferred_element_type=jnp.float32,
        ).astype(jnp.bfloat16)
        table_local.start()

    def step(s, carry):
        @pl.when(s < RX)
        def _():
            @pl.when(s > 0)
            def _():
                block_ready(s)

            produce_block(s)


        @pl.when(s == RX)
        def _():
            sibling_arrived(1).wait_recv()

        @pl.when((s >= RX) & (s < last))
        def _():
            produce(unit(s))

        @pl.when(s < RX - 1)
        def _():
            block_share(s + 1)

        @pl.when(s == 2)
        def _():
            build_codes()
            table_local.wait()
            peers(lambda i: table_copy(i).start())

        @pl.when(s == RX + 8)
        def _():
            build_routing()

        @pl.when((s >= LC) & (s < RX + LC))
        def _():
            combine_block(s - LC)

        @pl.when((s >= RX + LC) & (s < last + LC))
        def _():
            combine(unit(s - LC))

        @pl.when((s >= LF) & (s < RX + LF))
        def _():
            finish_block(s - LF)

        @pl.when(s >= RX + LF)
        def _():
            finish(unit(s - LF))

        @pl.when(s == RX - 2)
        def _():
            grad_share()

        return carry

    lax.fori_loop(0, last + LF, step, 0)

    for hop in range(1, RX):
        near_copy(hop).wait_send()

    def rows_sent(t, carry):
        for hop in range(RX):
            token_copy(0, place(t, hop)).wait_send()
        return carry

    lax.fori_loop(1, RX, rows_sent, 0)
    peers(lambda i: token_copy(1, i).wait_send())
    sibling_copy(1).wait_send()
    peers(lambda i: table_copy(i).wait_send())

    def x_sent(u, carry):
        for j in range(6):
            x_copy(u, j).wait_send()
        return carry

    def z_sent(m, carry):
        for j in range(6):
            z_copy(m, j).wait_send()
        return carry

    def b_sent(t, carry):
        @pl.when(t > 0)
        def _():
            block_copy(t, tokens.at[0, block_rows(t), columns]).wait_send()

        for j in range(6):
            b_copy(t, j).wait_send()
        return carry

    lax.fori_loop(0, RX, b_sent, 0)
    lax.fori_loop(RX, last, lambda s, carry: x_sent(unit(s), carry), 0)
    lax.fori_loop(0, 4, z_sent, 0)
    for h in range(2):
        out_local(h).wait()
        peers(lambda i, h=h: out_arrived(h, i).wait_recv())
        peers(lambda i, h=h: out_copy(h, i).wait_send())


def on_device(
    residual, cotangent, encoder_weight, encoder_bias, decoder_weight, route_experts, route_buckets
):
    features = encoder_bias.shape[0]
    hbm = pl.BlockSpec(memory_space=pltpu.HBM)
    dma = pltpu.SemaphoreType.DMA
    eighths = pl.pallas_call(
        kernel,
        out_shape=jax.ShapeDtypeStruct((E // NDP, features), jnp.float32),
        in_specs=[hbm] * 7,
        out_specs=hbm,
        scratch_shapes=[
            pltpu.VMEM((2, WIDE, features), jnp.bfloat16),
            pltpu.VMEM((2, NDP, OWN, 256), jnp.bfloat16),
            pltpu.VMEM((RX, OWN, WIDE), jnp.bfloat16),
            pltpu.VMEM((2, TOKENS, WIDE), jnp.bfloat16),
            pltpu.VMEM((NDP, OWN, HALF), jnp.bfloat16),
            pltpu.VMEM((1, features), jnp.float32),
            pltpu.VMEM((8, OWN), jnp.int32),
            pltpu.VMEM((8, OWN), jnp.int32),
            pltpu.VMEM((OWN, HALF), jnp.bfloat16),
            pltpu.VMEM((UNITS, 2, SPAN, HALF), jnp.float32),
            pltpu.VMEM((RX, 2, BLOCK, HALF), jnp.float32),
            pltpu.VMEM((UNITS, 2, SPAN, HALF), jnp.float32),
            pltpu.VMEM((TOKENS, HALF), jnp.float32),
            pltpu.VMEM((RX, 6, BLOCK + 8, HALF), jnp.int16),
            pltpu.VMEM((RX, 6, BLOCK + 8, HALF), jnp.int16),
            pltpu.VMEM((UNITS, 6, ROWS, HALF), jnp.int16),
            pltpu.VMEM((UNITS, 6, ROWS, HALF), jnp.int16),
            pltpu.VMEM((4, 6, ROWS, HALF), jnp.int16),
            pltpu.VMEM((4, 6, ROWS, HALF), jnp.int16),
            pltpu.VMEM((2, E, HALF), jnp.float32),
            pltpu.VMEM((E, TOKENS), jnp.bfloat16),
            dma((2,)),
            dma((6,)),
            dma((2, NDP)),
            dma((2, NDP)),
            dma((RX,)),
            dma((RX,)),
            dma((2,)),
            dma((2,)),
            dma((RX,)),
            dma((RX,)),
            dma((NDP,)),
            dma((NDP,)),
            dma((RX, 6)),
            dma((RX, 6)),
            dma((UNITS, 6)),
            dma((UNITS, 6)),
            dma((4, 6)),
            dma((4, 6)),
            dma((2, NDP)),
            dma((2, NDP)),
            dma((2,)),
        ],
        compiler_params=pltpu.CompilerParams(
            collective_id=0, has_side_effects=True, vmem_limit_bytes=56 * 1024 * 1024
        ),
        name="credit",
    )(
        residual,
        cotangent,
        encoder_weight,
        decoder_weight.T,
        encoder_bias.reshape(1, features),
        route_experts.T,
        route_buckets.T,
    )
    return eighths * 0.125


def solution(mesh):
    placed = (
        P("dp", None),
        P("dp", None),
        P("dp", "feat"),
        P("feat"),
        P("feat", "dp"),
        P("dp", None),
        P("dp", None),
    )
    return jax.shard_map(
        on_device, mesh=mesh, in_specs=placed, out_specs=P("dp", "feat"), check_vma=False
    )
```

```python
import functools

import jax
import jax.numpy as jnp
from jax import lax
from jax.experimental import pallas as pl
from jax.experimental.pallas import tpu as pltpu
from jax.sharding import PartitionSpec as P

TOKENS = 384
E = 256
RX = 4
NDP = 16
OWN = TOKENS // NDP
WIDE = 512
LIVE = 448
CHUNK = 256
HALF = 128
LC, LF = 1, 3
SPAN = TOKENS // 2
ROWS = SPAN + 8
UNITS = 16
BLOCK = TOKENS // RX
MESH = pl.DeviceIdType.MESH


def code(values):
    top = jnp.max(jnp.abs(values), axis=0, keepdims=True)
    step = jnp.ceil(jnp.log(jnp.maximum(top, 1e-30)) * 32.0)
    inverse = jnp.exp(step * (-1.0 / 32.0)) * 32000.0
    codes = jnp.round(values * inverse).astype(jnp.int32).astype(jnp.int16)
    steps = jnp.broadcast_to(step, (8, values.shape[1])).astype(jnp.int32).astype(jnp.int16)
    return codes, steps


def encode(values, ref):
    count = values.shape[0]
    ref[0:count, :], ref[count : count + 8, :] = code(values)


def encode_columns(values, first, second):
    count = values.shape[0]
    codes, steps = code(values)
    for n, ref in enumerate((first, second)):
        ref[0:count, :] = codes[:, n * HALF : (n + 1) * HALF]
        ref[count : count + 8, :] = steps[:, n * HALF : (n + 1) * HALF]


def encode_rows(values, first, second):
    count = values.shape[0] // 2
    codes, steps = code(values)
    for n, ref in enumerate((first, second)):
        ref[0:count, :] = codes[n * count : (n + 1) * count, :]
        ref[count : count + 8, :] = steps


def decode(ref):
    count = ref.shape[0] - 8
    step = ref[count : count + 8, :].astype(jnp.int32).astype(jnp.float32)[0:1, :]
    scale = jnp.exp(step * (1.0 / 32.0)) * (1.0 / 32000.0)
    return ref[0:count, :].astype(jnp.int32).astype(jnp.float32) * scale


def window_start(d):
    return 896 * (d // 2) + 384 * (d % 2)


def kernel(
    residual,
    cotangent,
    encoder,
    decoder,
    bias_hbm,
    experts_hbm,
    buckets_hbm,
    out,
    weights,
    landing,
    first,
    tokens,
    table,
    bias,
    experts,
    buckets,
    codes,
    near,
    near_block,
    own,
    active,
    bsend,
    brecv,
    xsend,
    xrecv,
    zsend,
    zrecv,
    credit,
    routing,
    w_sem,
    l_sem,
    tok_send,
    tok_recv,
    near_send,
    near_recv,
    sib_send,
    sib_recv,
    sibb_send,
    sibb_recv,
    tab_send,
    tab_recv,
    bs_sem,
    br_sem,
    xs_sem,
    xr_sem,
    zs_sem,
    zr_sem,
    out_send,
    out_recv,
    out_sem,
):
    me = lax.axis_index("dp")
    feat = lax.axis_index("feat")
    core = feat % 2
    sibling = feat + 1 - 2 * core
    x = me % RX
    z = me // RX
    off = 64 * (me % 2)

    x_left = z * RX + (x + 3) % RX
    x_right = z * RX + (x + 1) % RX
    z_left = ((z + 3) % RX) * RX + x
    z_right = ((z + 1) % RX) * RX + x

    def weight_copy(m):
        source = encoder if m == 0 else decoder
        return pltpu.make_async_copy(
            source, weights.at[m, pl.ds(pl.multiple_of(off, 64), LIVE), :], w_sem.at[m]
        )

    for m in range(2):
        weight_copy(m).start()

    columns = pl.ds(pl.multiple_of(core * 256, 256), 256)

    def token_source(m, d):
        source = residual if m == 0 else cotangent
        return source.at[:, pl.ds(pl.multiple_of(window_start(d) + core * 256, 128), 256)]

    def token_local(m):
        return pltpu.make_async_copy(token_source(m, me), landing.at[m, me], l_sem.at[m])

    def first_local():
        return pltpu.make_async_copy(
            residual.at[:, pl.ds(pl.multiple_of(window_start(me), 128), WIDE)],
            first.at[x],
            l_sem.at[0],
        )

    small = [
        pltpu.make_async_copy(source, target, l_sem.at[3 + n])
        for n, (source, target) in enumerate(
            ((bias_hbm, bias), (experts_hbm, experts), (buckets_hbm, buckets))
        )
    ]
    first_local().start()
    token_local(1).start()
    for copy in small:
        copy.start()

    barrier = pltpu.get_barrier_semaphore()

    def greet(i, carry):
        pl.semaphore_signal(
            barrier, inc=1, device_id={"dp": (me + i) % NDP}, device_id_type=MESH
        )
        return carry

    lax.fori_loop(1, NDP, greet, 0)
    pl.semaphore_signal(barrier, inc=1, device_id={"feat": sibling}, device_id_type=MESH)
    pl.semaphore_wait(barrier, NDP)

    def token_copy(m, i):
        d = (me + i) % NDP
        return pltpu.make_async_remote_copy(
            src_ref=token_source(m, d),
            dst_ref=landing.at[m, me],
            send_sem=tok_send.at[m, i],
            recv_sem=tok_recv.at[m, i],
            device_id={"dp": d},
            device_id_type=MESH,
        )

    def near_source(d):
        return residual.at[:, pl.ds(pl.multiple_of(window_start(d), 128), WIDE)]

    def near_copy(hop):
        d = z * RX + (x + hop) % RX
        return pltpu.make_async_remote_copy(
            src_ref=near_source(d),
            dst_ref=first.at[x],
            send_sem=near_send.at[hop],
            recv_sem=near_recv.at[hop],
            device_id={"dp": d},
            device_id_type=MESH,
        )

    def near_arrived(hop):
        s = (x + RX - hop) % RX
        return pltpu.make_async_remote_copy(
            src_ref=first.at[s],
            dst_ref=first.at[s],
            send_sem=near_send.at[hop],
            recv_sem=near_recv.at[hop],
            device_id={"dp": z * RX + s},
            device_id_type=MESH,
        )

    def sibling_copy(m):
        part = tokens.at[m, :, columns]
        return pltpu.make_async_remote_copy(
            src_ref=part,
            dst_ref=part,
            send_sem=sib_send.at[m],
            recv_sem=sib_recv.at[m],
            device_id={"feat": sibling},
            device_id_type=MESH,
        )

    def sibling_arrived(m):
        part = tokens.at[m, :, pl.ds(pl.multiple_of(256 - core * 256, 256), 256)]
        return pltpu.make_async_remote_copy(
            src_ref=part,
            dst_ref=part,
            send_sem=sib_send.at[m],
            recv_sem=sib_recv.at[m],
            device_id={"feat": sibling},
            device_id_type=MESH,
        )

    def token_arrived(m, i):
        s = (me + NDP - i) % NDP
        part = landing.at[m, s]
        return pltpu.make_async_remote_copy(
            src_ref=part,
            dst_ref=part,
            send_sem=tok_send.at[m, i],
            recv_sem=tok_recv.at[m, i],
            device_id={"dp": s},
            device_id_type=MESH,
        )

    def table_copy(i):
        d = (me + i) % NDP
        return pltpu.make_async_remote_copy(
            src_ref=codes,
            dst_ref=table.at[me],
            send_sem=tab_send.at[i],
            recv_sem=tab_recv.at[i],
            device_id={"dp": d},
            device_id_type=MESH,
        )

    def table_arrived(i):
        s = (me + NDP - i) % NDP
        part = table.at[s]
        return pltpu.make_async_remote_copy(
            src_ref=part,
            dst_ref=part,
            send_sem=tab_send.at[i],
            recv_sem=tab_recv.at[i],
            device_id={"dp": s},
            device_id_type=MESH,
        )

    def peers(action):
        def step(i, carry):
            action(i)
            return carry

        lax.fori_loop(1, NDP, step, 0)

    def row_offset(t):
        return t + t // 2 - 2 * (t // 3)

    def place(t, hop):
        d = ((z + row_offset(t)) % RX) * RX + (x + hop) % RX
        return (d + NDP - me) % NDP

    def send_tokens(m):
        for hop in range(1, RX):
            near_copy(hop).start() if m == 0 else token_copy(m, place(0, hop)).start()

        def send_row(t, carry):
            for hop in range(RX):
                token_copy(m, place(t, hop)).start()
            return carry

        lax.fori_loop(1, RX, send_row, 0)

    send_tokens(0)
    send_tokens(1)

    blank = pl.ds(pl.multiple_of(LIVE - LIVE * (me % 2), 64), 64)
    for m in range(2):
        weights[m, blank, :] = jnp.zeros((64, weights.shape[2]), jnp.bfloat16)

    def block_rows(t):
        return pl.ds(pl.multiple_of(((z + row_offset(t)) % RX) * BLOCK, BLOCK), BLOCK)

    def block_copy(t, part):
        return pltpu.make_async_remote_copy(
            src_ref=part,
            dst_ref=part,
            send_sem=sibb_send.at[t],
            recv_sem=sibb_recv.at[t],
            device_id={"feat": sibling},
            device_id_type=MESH,
        )

    theirs = pl.ds(pl.multiple_of(256 - core * 256, 256), 256)

    def block_share(t):
        row = (z + row_offset(t)) % RX
        for hop in range(RX):
            s = row * RX + (x + hop) % RX
            token_arrived(0, (me + NDP - s) % NDP).wait_recv()
        rows = landing[0, pl.ds(row * RX, RX)].astype(jnp.float32).reshape(BLOCK, 256)
        tokens[0, block_rows(t), columns] = rows.astype(jnp.bfloat16)
        block_copy(t, tokens.at[0, block_rows(t), columns]).start()

    def first_ready():
        first_local().wait()
        for hop in range(1, RX):
            near_arrived(hop).wait_recv()
        rows = first[...].astype(jnp.float32).reshape(BLOCK, WIDE)
        tokens[0, block_rows(0), :] = rows.astype(jnp.bfloat16)

    def block_ready(t):
        block_copy(t, tokens.at[0, block_rows(t), theirs]).wait_recv()

    def grad_share():
        token_local(1).wait()
        peers(lambda i: token_arrived(1, i).wait_recv())
        rows = landing[1].astype(jnp.float32).reshape(TOKENS, 256)
        tokens[1, :, columns] = rows.astype(jnp.bfloat16)
        sibling_copy(1).start()

    def x_copy(u, j):
        return pltpu.make_async_remote_copy(
            src_ref=xsend.at[u, j],
            dst_ref=xrecv.at[u, j],
            send_sem=xs_sem.at[u, j],
            recv_sem=xr_sem.at[u, j],
            device_id={"dp": x_left if j % 2 == 0 else x_right},
            device_id_type=MESH,
        )

    def b_copy(t, j):
        return pltpu.make_async_remote_copy(
            src_ref=bsend.at[t, j],
            dst_ref=brecv.at[t, j],
            send_sem=bs_sem.at[t, j],
            recv_sem=br_sem.at[t, j],
            device_id={"dp": x_left if j % 2 == 0 else x_right},
            device_id_type=MESH,
        )

    def z_copy(m, j):
        return pltpu.make_async_remote_copy(
            src_ref=zsend.at[m, j],
            dst_ref=zrecv.at[m, j],
            send_sem=zs_sem.at[m, j],
            recv_sem=zr_sem.at[m, j],
            device_id={"dp": z_left if j % 2 == 0 else z_right},
            device_id_type=MESH,
        )

    def b_copy(t, j):
        return pltpu.make_async_remote_copy(
            src_ref=bsend.at[t, j],
            dst_ref=brecv.at[t, j],
            send_sem=bs_sem.at[t, j],
            recv_sem=br_sem.at[t, j],
            device_id={"dp": x_left if j % 2 == 0 else x_right},
            device_id_type=MESH,
        )

    def b_send(t, j, values):
        encode(values, bsend.at[t, j])
        b_copy(t, j).start()

    def z_copy(m, j):
        return pltpu.make_async_remote_copy(
            src_ref=zsend.at[m, j],
            dst_ref=zrecv.at[m, j],
            send_sem=zs_sem.at[m, j],
            recv_sem=zr_sem.at[m, j],
            device_id={"dp": z_left if j % 2 == 0 else z_right},
            device_id_type=MESH,
        )

    def x_send(u, j, values):
        encode(values, xsend.at[u, j])
        x_copy(u, j).start()

    def z_send(m, j, values):
        encode(values, zsend.at[m, j])
        z_copy(m, j).start()

    spans = (pl.ds(0, SPAN), pl.ds(SPAN, SPAN))

    def produce(u):
        k, h, m = u // 4, (u // 2) % 2, u % 2
        back = 3 - k
        row = (z + ((back + 1) % 3 + 1) * ((back + 3) // 4)) % RX

        def partial(hop):
            first = (row * RX + (x + hop) % RX) * CHUNK + h * HALF
            return jnp.dot(
                tokens[m],
                weights[m, :, pl.ds(pl.multiple_of(first, HALF), HALF)],
                preferred_element_type=jnp.float32,
            )

        encode_rows(partial(2), xsend.at[u, 0], xsend.at[u, 1])
        x_copy(u, 0).start()
        x_copy(u, 1).start()
        left, right = partial(3), partial(1)
        encode_columns(
            jnp.concatenate([left[SPAN:], right[:SPAN]], axis=1), xsend.at[u, 2], xsend.at[u, 3]
        )
        x_copy(u, 2).start()
        x_copy(u, 3).start()
        near[u, 0] = left[:SPAN]
        near[u, 1] = right[SPAN:]
        mine = partial(0)
        own[u, 0] = mine[:SPAN]
        own[u, 1] = mine[SPAN:]

    def block_place(t):
        row = (z + row_offset(t)) % RX
        return row // 2, pl.ds(pl.multiple_of((row % 2) * BLOCK, BLOCK), BLOCK)

    def produce_block(t):
        row = (z + 2) % RX

        def partial(hop):
            first = (row * RX + (x + hop) % RX) * CHUNK
            return jnp.dot(
                tokens[0, block_rows(t), :],
                weights[0, :, pl.ds(pl.multiple_of(first, CHUNK), CHUNK)],
                preferred_element_type=jnp.float32,
            )

        encode_columns(partial(2), bsend.at[t, 0], bsend.at[t, 1])
        b_copy(t, 0).start()
        b_copy(t, 1).start()
        left, right = partial(3), partial(1)
        encode_columns(
            jnp.concatenate([left[:, HALF:], right[:, :HALF]], axis=1),
            bsend.at[t, 2],
            bsend.at[t, 3],
        )
        b_copy(t, 2).start()
        b_copy(t, 3).start()
        near_block[t, 0] = left[:, :HALF]
        near_block[t, 1] = right[:, HALF:]
        mine = partial(0)
        span, rows = block_place(t)
        own[0, span, rows, :] = mine[:, :HALF]
        own[2, span, rows, :] = mine[:, HALF:]

    def combine_block(t):
        for j in range(2):
            b_copy(t, j).wait_recv()
        encode_columns(
            jnp.concatenate(
                [near_block[t, j] + decode(brecv.at[t, j]) for j in range(2)], axis=1
            ),
            bsend.at[t, 4],
            bsend.at[t, 5],
        )
        b_copy(t, 4).start()
        b_copy(t, 5).start()

    def finish_block(t):
        for j in range(2, 6):
            b_copy(t, j).wait_recv()
        span, rows = block_place(t)
        own[0, span, rows, :] += decode(brecv.at[t, 4]) + decode(brecv.at[t, 3])
        own[2, span, rows, :] += decode(brecv.at[t, 5]) + decode(brecv.at[t, 2])

        @pl.when(t == RX - 1)
        def _():
            for q in (0, 2):
                z_send(q, 0, own[q, 0])
                z_send(q, 1, own[q, 1])

    def combine(u):
        for j in range(2):
            x_copy(u, j).wait_recv()
        encode_columns(
            jnp.concatenate([near[u, j] + decode(xrecv.at[u, j]) for j in range(2)], axis=1),
            xsend.at[u, 4],
            xsend.at[u, 5],
        )
        x_copy(u, 4).start()
        x_copy(u, 5).start()

    def finish(u):
        k, q = u // 4, u % 4
        for j in range(2, 4):
            x_copy(u, j).wait_recv()
        own[u, 0] += decode(xrecv.at[u, 3])
        own[u, 1] += decode(xrecv.at[u, 2])

        @pl.when(k == 3)
        def _():
            for j in range(2, 6):
                z_copy(q, j).wait_recv()
            own[u, 0] += decode(zrecv.at[q, 4]) + decode(zrecv.at[q, 3])
            own[u, 1] += decode(zrecv.at[q, 5]) + decode(zrecv.at[q, 2])

        for j in range(4, 6):
            x_copy(u, j).wait_recv()
        own[u, 0] += decode(xrecv.at[u, 4])
        own[u, 1] += decode(xrecv.at[u, 5])

        @pl.when(k == 0)
        def _():
            z_send(q, 0, own[u, 0])
            z_send(q, 1, own[u, 1])

        @pl.when(k == 1)
        def _():
            z_send(q, 3, own[u, 0])
            z_copy(q, 1).wait_recv()
            z_send(q, 5, own[u, 1] + decode(zrecv.at[q, 1]))

        @pl.when(k == 2)
        def _():
            z_send(q, 2, own[u, 1])
            z_copy(q, 0).wait_recv()
            z_send(q, 4, own[u, 0] + decode(zrecv.at[q, 0]))

        @pl.when((k == 3) & (q % 2 == 0))
        def _():
            mine = pl.ds(pl.multiple_of(me * CHUNK + (q // 2) * HALF, HALF), HALF)
            for n in range(2):
                active[spans[n], :] = jnp.maximum(own[u, n] + bias[:, mine], 0.0)

        @pl.when((k == 3) & (q % 2 == 1))
        def _():
            deliver(u, q // 2)

    def build_routing():
        peers(lambda i: table_arrived(i).wait_recv())
        values = table[...].astype(jnp.float32).reshape(TOKENS, HALF).T
        names = lax.broadcasted_iota(jnp.int32, (E, TOKENS), 0).astype(jnp.float32)
        total = jnp.zeros((E, TOKENS), jnp.float32)
        for k in range(8):
            total += jnp.where(values[k : k + 1, :] == names, values[8 + k : 9 + k, :], 0.0)
        routing[...] = total.astype(jnp.bfloat16)

    def out_copy(h, i):
        d = (me + i) % NDP
        return pltpu.make_async_remote_copy(
            src_ref=credit.at[h, pl.ds(pl.multiple_of(d * 16, 16), 16), :],
            dst_ref=out.at[:, pl.ds(pl.multiple_of(me * CHUNK + h * HALF, HALF), HALF)],
            send_sem=out_send.at[h, i],
            recv_sem=out_recv.at[h, i],
            device_id={"dp": d},
            device_id_type=MESH,
        )

    def out_local(h):
        return pltpu.make_async_copy(
            credit.at[h, pl.ds(pl.multiple_of(me * 16, 16), 16), :],
            out.at[:, pl.ds(pl.multiple_of(me * CHUNK + h * HALF, HALF), HALF)],
            out_sem.at[h],
        )

    def out_arrived(h, i):
        s = (me + NDP - i) % NDP
        part = out.at[:, pl.ds(pl.multiple_of(s * CHUNK + h * HALF, HALF), HALF)]
        return pltpu.make_async_remote_copy(
            src_ref=part,
            dst_ref=part,
            send_sem=out_send.at[h, i],
            recv_sem=out_recv.at[h, i],
            device_id={"dp": s},
            device_id_type=MESH,
        )

    def deliver(u, h):
        mine = pl.ds(pl.multiple_of(me * CHUNK + h * HALF, HALF), HALF)
        score = active[...] * jnp.concatenate([own[u, 0], own[u, 1]], axis=0)
        high = score.astype(jnp.bfloat16)
        low = (score - high.astype(jnp.float32)).astype(jnp.bfloat16)
        credit[h] = jnp.dot(
            routing[...], high, preferred_element_type=jnp.float32
        ) + jnp.dot(routing[...], low, preferred_element_type=jnp.float32)
        for t in (3, 1, 2, 0):
            for hop in range(RX):
                if t + hop > 0:
                    out_copy(h, place(t, hop)).start()
        out_local(h).start()

    def unit(s):
        n = s - RX
        return n + 1 + (n + 13) // 14

    last = RX + UNITS - 2
    for m in range(2):
        weight_copy(m).wait()
    first_ready()

    table_local = pltpu.make_async_copy(codes, table.at[me], l_sem.at[2])

    def build_codes():
        for copy in small:
            copy.wait()
        codes[...] = jnp.zeros_like(codes)
        named = experts[...].astype(jnp.float32)
        weight = buckets[...].astype(jnp.float32)
        both = jnp.concatenate([named, weight], axis=0).astype(jnp.bfloat16)
        same = lax.broadcasted_iota(jnp.int32, (OWN, OWN), 0) == lax.broadcasted_iota(
            jnp.int32, (OWN, OWN), 1
        )
        codes[:, 0:16] = lax.dot_general(
            jnp.where(same, 1.0, 0.0).astype(jnp.bfloat16),
            both,
            (((1,), (1,)), ((), ())),
            preferred_element_type=jnp.float32,
        ).astype(jnp.bfloat16)
        table_local.start()

    def step(s, carry):
        @pl.when(s < RX)
        def _():
            @pl.when(s > 0)
            def _():
                block_ready(s)

            produce_block(s)


        @pl.when(s == RX)
        def _():
            sibling_arrived(1).wait_recv()

        @pl.when((s >= RX) & (s < last))
        def _():
            produce(unit(s))

        @pl.when(s == 2)
        def _():
            build_codes()
            table_local.wait()
            peers(lambda i: table_copy(i).start())

        @pl.when(s == RX + 8)
        def _():
            build_routing()

        @pl.when((s >= LC) & (s < RX + LC))
        def _():
            combine_block(s - LC)

        @pl.when((s >= RX + LC) & (s < last + LC))
        def _():
            combine(unit(s - LC))

        @pl.when(s < RX - 1)
        def _():
            block_share(s + 1)

        @pl.when((s >= LF) & (s < RX + LF))
        def _():
            finish_block(s - LF)

        @pl.when(s >= RX + LF)
        def _():
            finish(unit(s - LF))

        @pl.when(s == RX - 2)
        def _():
            grad_share()

        return carry

    lax.fori_loop(0, last + LF, step, 0)

    for hop in range(1, RX):
        near_copy(hop).wait_send()

    def rows_sent(t, carry):
        for hop in range(RX):
            token_copy(0, place(t, hop)).wait_send()
        return carry

    lax.fori_loop(1, RX, rows_sent, 0)
    peers(lambda i: token_copy(1, i).wait_send())
    sibling_copy(1).wait_send()
    peers(lambda i: table_copy(i).wait_send())

    def x_sent(u, carry):
        for j in range(6):
            x_copy(u, j).wait_send()
        return carry

    def z_sent(m, carry):
        for j in range(6):
            z_copy(m, j).wait_send()
        return carry

    def b_sent(t, carry):
        @pl.when(t > 0)
        def _():
            block_copy(t, tokens.at[0, block_rows(t), columns]).wait_send()

        for j in range(6):
            b_copy(t, j).wait_send()
        return carry

    lax.fori_loop(0, RX, b_sent, 0)
    lax.fori_loop(RX, last, lambda s, carry: x_sent(unit(s), carry), 0)
    lax.fori_loop(0, 4, z_sent, 0)
    for h in range(2):
        out_local(h).wait()
        peers(lambda i, h=h: out_arrived(h, i).wait_recv())
        peers(lambda i, h=h: out_copy(h, i).wait_send())


def on_device(
    residual, cotangent, encoder_weight, encoder_bias, decoder_weight, route_experts, route_buckets
):
    features = encoder_bias.shape[0]
    hbm = pl.BlockSpec(memory_space=pltpu.HBM)
    dma = pltpu.SemaphoreType.DMA
    eighths = pl.pallas_call(
        kernel,
        out_shape=jax.ShapeDtypeStruct((E // NDP, features), jnp.float32),
        in_specs=[hbm] * 7,
        out_specs=hbm,
        scratch_shapes=[
            pltpu.VMEM((2, WIDE, features), jnp.bfloat16),
            pltpu.VMEM((2, NDP, OWN, 256), jnp.bfloat16),
            pltpu.VMEM((RX, OWN, WIDE), jnp.bfloat16),
            pltpu.VMEM((2, TOKENS, WIDE), jnp.bfloat16),
            pltpu.VMEM((NDP, OWN, HALF), jnp.bfloat16),
            pltpu.VMEM((1, features), jnp.float32),
            pltpu.VMEM((8, OWN), jnp.int32),
            pltpu.VMEM((8, OWN), jnp.int32),
            pltpu.VMEM((OWN, HALF), jnp.bfloat16),
            pltpu.VMEM((UNITS, 2, SPAN, HALF), jnp.float32),
            pltpu.VMEM((RX, 2, BLOCK, HALF), jnp.float32),
            pltpu.VMEM((UNITS, 2, SPAN, HALF), jnp.float32),
            pltpu.VMEM((TOKENS, HALF), jnp.float32),
            pltpu.VMEM((RX, 6, BLOCK + 8, HALF), jnp.int16),
            pltpu.VMEM((RX, 6, BLOCK + 8, HALF), jnp.int16),
            pltpu.VMEM((UNITS, 6, ROWS, HALF), jnp.int16),
            pltpu.VMEM((UNITS, 6, ROWS, HALF), jnp.int16),
            pltpu.VMEM((4, 6, ROWS, HALF), jnp.int16),
            pltpu.VMEM((4, 6, ROWS, HALF), jnp.int16),
            pltpu.VMEM((2, E, HALF), jnp.float32),
            pltpu.VMEM((E, TOKENS), jnp.bfloat16),
            dma((2,)),
            dma((6,)),
            dma((2, NDP)),
            dma((2, NDP)),
            dma((RX,)),
            dma((RX,)),
            dma((2,)),
            dma((2,)),
            dma((RX,)),
            dma((RX,)),
            dma((NDP,)),
            dma((NDP,)),
            dma((RX, 6)),
            dma((RX, 6)),
            dma((UNITS, 6)),
            dma((UNITS, 6)),
            dma((4, 6)),
            dma((4, 6)),
            dma((2, NDP)),
            dma((2, NDP)),
            dma((2,)),
        ],
        compiler_params=pltpu.CompilerParams(
            collective_id=0, has_side_effects=True, vmem_limit_bytes=56 * 1024 * 1024
        ),
        name="credit",
    )(
        residual,
        cotangent,
        encoder_weight,
        decoder_weight.T,
        encoder_bias.reshape(1, features),
        route_experts.T,
        route_buckets.T,
    )
    return eighths * 0.125


def solution(mesh):
    placed = (
        P("dp", None),
        P("dp", None),
        P("dp", "feat"),
        P("feat"),
        P("feat", "dp"),
        P("dp", None),
        P("dp", None),
    )
    return jax.shard_map(
        on_device, mesh=mesh, in_specs=placed, out_specs=P("dp", "feat"), check_vma=False
    )
```
